256 devices in a mesh: ctx: 32 (over x_hi, z, core), tp: 8 (over x_lo, y).
Axes of the slice: x: 4 (x_hi: 2, x_lo: 2; x = x_hi * 2 + x_lo), y: 4, z: 8, core: 2. Of those that a mesh axis runs over, the one named last changes fastest.
Arguments:
- queries: bfloat16 [64, 3, 128, 128], P('ctx', None, 'tp'), may hold values from -480 to 480
- prefix_keys: bfloat16 [65536, 8, 128], P('ctx', 'tp'), may hold values from -6 to 6
- prefix_values: bfloat16 [65536, 8, 128], P('ctx', 'tp'), may hold values from -6 to 6
- suffix_keys: bfloat16 [64, 512, 8, 128], P('ctx', None, 'tp'), may hold values from -6 to 6
- suffix_values: bfloat16 [64, 512, 8, 128], P('ctx', None, 'tp'), may hold values from -6 to 6
- fork_lengths: int32 [64], P('ctx'), may hold values from 1 to 509, 16384 in all
- out_weight: bfloat16 [16384, 16384], P('tp', 'ctx'), may hold values from -0.046875 to 0.046875
Outputs:
- projected: bfloat16 [64, 3, 16384], P('tp', None, 'ctx')
The draws below stay inside these ranges and needn't reach their ends.
Inputs may be any that keep to these rules, and one draw needn't show every extreme that they name: `fork_lengths`: A fork's earlier tokens fill the first slots of its suffix, followed by the keys and values of its 3 new tokens.
All inputs are finite; a program needn't handle non-finite values. No bound on the sum of `fork_lengths` on one device may be relied on, other than what follows from the above.
Results may differ from the reference program's by a relative error of at most 0.014.
Values may be sent and summed in bfloat16 or wider, within the bound.
No kernel may reach another device: no remote copies, remote signals or barrier semaphores. Data moves between devices by JAX's collectives and lax.ppermute only.
A program may use at most 64 MiB of HBM per device.

```python
import math
import jax
import jax.numpy as jnp
import numpy as np
from jax import lax

D = 16384
HEADS = 128
KV_HEADS = 8
HD = 128
PRE_DEV = 2048
SUF_MAX = 512
STEPS = 3
FORKS = 64
PREFIX = 65536
N_CTX = 32


def draw_queries(key, part):
    shape = (FORKS, STEPS, HEADS, HD)
    base_key = jax.random.fold_in(jax.random.fold_in(key, 11), 0)
    entries = jnp.clip(jax.random.normal(base_key, shape, jnp.float32), -6.0, 6.0)
    return entries.astype(jnp.bfloat16)


def block_levels(key, dims, cuts, least, largest):
    loudness, own = 1.0, jax.random.fold_in(key, 6)
    for axis_at, shards_of in cuts:
        draws = jnp.exp(jax.random.uniform(jax.random.fold_in(own, axis_at), (shards_of,), jnp.float32, least / len(cuts), largest / len(cuts)))
        loudness = loudness * jnp.repeat(draws, dims[axis_at] // shards_of).reshape([-1 if axis == axis_at else 1 for axis in range(len(dims))])
    return loudness


def length_profile(count, total, reach, slope):
    weights = [(1 << 20) // math.isqrt(standing ** slope) + 1 for standing in range(2, count + 1)]
    spare, given = total - reach - (count - 1), [1] * (count - 1)
    while spare > 0:
        candidates = [i for i in range(count - 1) if given[i] < reach]
        pool, left = sum([weights[i] for i in candidates]), spare
        for i in candidates:
            addition = min(reach - given[i], max(1, left * weights[i] // pool), spare)
            given[i] = given[i] + addition
            spare = spare - addition
    return np.array([reach] + given)


def ragged(key, amount, total, bound, slope):
    if amount == 2:
        one = jax.random.randint(key, (), max(1, total - bound), min(bound, total - 1) + 1)
        return jnp.stack([one, total - one])
    lengths = jnp.asarray(length_profile(amount, total, bound, slope), jnp.int32)
    couples = (amount - 1) // 2
    donor, sink = lengths[1:1 + 2 * couples:2], lengths[2:2 + 2 * couples:2]
    margin = jnp.minimum(donor - 1, bound - sink)
    moved = jax.random.randint(jax.random.fold_in(key, 1), (couples,), 0, 1 << 20) % (margin + 1)
    lengths = lengths.at[1:1 + 2 * couples:2].set(donor - moved).at[2:2 + 2 * couples:2].set(sink + moved)
    return lengths[jax.random.permutation(jax.random.fold_in(key, 2), amount)]


def gaussian(own_key, dims, spread, most, cuts=(), kind=jnp.bfloat16):
    factor_of = block_levels(own_key, dims, cuts, -0.22, 0.18) if cuts else 1.0
    values = jax.random.normal(own_key, dims, jnp.float32) * spread * factor_of
    return jnp.minimum(jnp.maximum(values, -most), most).astype(kind)


def setup_inputs(seed: int = 0) -> dict:
    seeds = jax.random.split(jax.random.key(seed), 8)
    queries = draw_queries(jax.random.fold_in(seeds[7], 71), 0)
    prefix_keys = gaussian(seeds[1], (PREFIX, KV_HEADS, HD), 1.0, 6.0, ((0, 32), (1, 8)))
    prefix_values = gaussian(seeds[2], (PREFIX, KV_HEADS, HD), 1.0, 6.0, ((0, 32), (1, 8)))
    suffix_keys = gaussian(seeds[3], (FORKS, SUF_MAX, KV_HEADS, HD), 1.0, 6.0, ((0, 32), (2, 8)))
    suffix_values = gaussian(seeds[4], (FORKS, SUF_MAX, KV_HEADS, HD), 1.0, 6.0, ((0, 32), (2, 8)))
    fork_lengths = ragged(seeds[5], FORKS, FORKS * (SUF_MAX // 2), SUF_MAX - STEPS, 2).astype(jnp.int32)
    out_weight = gaussian(seeds[6], (HEADS * HD, D), (HEADS * HD) ** -0.5, 0.046875, ((0, 8), (1, 32)))
    return dict(queries=queries, prefix_keys=prefix_keys, prefix_values=prefix_values, suffix_keys=suffix_keys, suffix_values=suffix_values, fork_lengths=fork_lengths, out_weight=out_weight)


def combine(first, second):
    mixed_a, highest_a, totals_a = first
    mixed_b, highest_b, totals_b = second
    summit = jnp.maximum(highest_a, highest_b)
    factor_a = jnp.exp(highest_a - summit)
    factor_b = jnp.exp(highest_b - summit)
    mixed = mixed_a * factor_a[..., None] + mixed_b * factor_b[..., None]
    return (mixed, summit, totals_a * factor_a + totals_b * factor_b)


def softmax_state(scores, values, form, shape):
    highest = jnp.max(scores, axis=-1)
    weights = jnp.exp(scores - highest[..., None])
    totals = jnp.sum(weights, axis=-1)
    mixed = jnp.einsum(form, weights.astype(jnp.bfloat16).astype(jnp.float32), values.astype(jnp.float32))
    return (mixed.reshape(shape), highest.reshape(shape[:3]), totals.reshape(shape[:3]))


def reference(queries, prefix_keys, prefix_values, suffix_keys, suffix_values, fork_lengths, out_weight):
    group = HEADS // KV_HEADS
    scale = HD ** -0.5
    width = math.gcd(FORKS, 16)
    blocks = FORKS // width

    def per_block(items):
        block_queries, block_keys, block_values, block_lengths = items
        shape = block_queries.shape
        grouped = block_queries.astype(jnp.float32).reshape(width, STEPS, KV_HEADS, group, HD)
        state = None
        for segment in range(N_CTX):
            seg_keys = prefix_keys[segment * PRE_DEV:(segment + 1) * PRE_DEV].astype(jnp.float32)
            seg_values = prefix_values[segment * PRE_DEV:(segment + 1) * PRE_DEV]
            scores = jnp.einsum("bskgd,pkd->bskgp", grouped, seg_keys) * scale
            partial_state = softmax_state(scores, seg_values, "bskgp,pkd->bskgd", shape)
            state = partial_state if state is None else combine(state, partial_state)
        scores = jnp.einsum("bskgd,bpkd->bskgp", grouped, block_keys.astype(jnp.float32)) * scale
        limit = block_lengths[:, None] + jnp.arange(STEPS, dtype=jnp.int32)[None, :] + 1
        visible = jnp.arange(SUF_MAX, dtype=jnp.int32)[None, None, :] < limit[:, :, None]
        scores = jnp.where(visible[:, :, None, None, :], scores, jnp.float32(-1e30))
        state = combine(state, softmax_state(scores, block_values, "bskgp,bpkd->bskgd", shape))
        mixed, highest, totals = state
        return (mixed / totals[..., None]).astype(jnp.bfloat16)

    attention = lax.map(per_block, (
        queries.reshape(blocks, width, STEPS, HEADS, HD),
        suffix_keys.reshape(blocks, width, SUF_MAX, KV_HEADS, HD),
        suffix_values.reshape(blocks, width, SUF_MAX, KV_HEADS, HD),
        fork_lengths.reshape(blocks, width)))
    rows = attention.reshape(FORKS * STEPS, HEADS * HD)
    result = jnp.dot(rows, out_weight, preferred_element_type=jnp.float32).astype(jnp.bfloat16)
    return result.reshape(FORKS, STEPS, D)
```

```python
import functools

import jax
import jax.numpy as jnp
from jax import lax
from jax.experimental import pallas as pl
from jax.experimental.pallas import tpu as pltpu
from jax.sharding import Mesh
from jax.sharding import PartitionSpec as P

CTX = ("xh", "z", "core")
CHIPS = ("xh", "z")
TP = ("xl", "y")
STATS = 8
NEG = -1e30
LOG2E = 1.4426950408889634
VMEM = pltpu.VMEM


def dot(a, b, ca, cb):
    return lax.dot_general(
        a, b, (((ca,), (cb,)), ((), ())), preferred_element_type=jnp.float32
    )


def shift_of(scores_max):
    hi = scores_max.astype(jnp.bfloat16)
    lo = (scores_max - hi.astype(jnp.float32)).astype(jnp.bfloat16)
    return hi, lo, hi.astype(jnp.float32) + lo.astype(jnp.float32)


def stat_rows(hi, lo, totals):
    rows = hi.shape[0]
    t_hi = totals.astype(jnp.bfloat16)
    t_lo = (totals - t_hi.astype(jnp.float32)).astype(jnp.bfloat16)
    lane = lax.broadcasted_iota(jnp.int32, (rows, 128), 1)
    f = jnp.float32
    table = jnp.where(
        lane == 0,
        hi.astype(f),
        jnp.where(
            lane == 1,
            lo.astype(f),
            jnp.where(lane == 2, t_hi.astype(f), jnp.where(lane == 3, t_lo.astype(f), 0.0)),
        ),
    ).astype(jnp.bfloat16)
    if rows < 128:
        table = jnp.concatenate([table, jnp.zeros((128 - rows, 128), jnp.bfloat16)], axis=0)
    pick = (
        lax.broadcasted_iota(jnp.int32, (STATS, 128), 0)
        == lax.broadcasted_iota(jnp.int32, (STATS, 128), 1)
    ).astype(jnp.bfloat16)
    return dot(pick, table, 1, 1).astype(jnp.bfloat16)


def prefix_kernel(c, q_ref, ko_ref, kp_ref, vo_ref, vp_ref, out_ref, v_ref):
    n_seg, rows, hd = q_ref.shape
    keys = ko_ref.shape[0]

    @pl.when(pl.program_id(0) == 0)
    def _():
        v_ref[:keys, :hd] = vo_ref[...]
        v_ref[keys:, :hd] = vp_ref[...]
        v_ref[:, hd:] = jnp.ones((2 * keys, hd), jnp.bfloat16)

    q = q_ref[...].reshape(n_seg * rows, hd)
    s1 = dot(q, ko_ref[...], 1, 1)
    s2 = dot(q, kp_ref[...], 1, 1)
    top = jnp.maximum(
        jnp.max(s1, axis=1, keepdims=True), jnp.max(s2, axis=1, keepdims=True)
    )
    hi, lo, shift = shift_of(top)
    p1 = jnp.exp2((s1 - shift) * c).astype(jnp.bfloat16)
    p2 = jnp.exp2((s2 - shift) * c).astype(jnp.bfloat16)
    o = dot(p1, v_ref[:keys], 1, 0) + dot(p2, v_ref[keys:], 1, 0)
    mixed = o[:, :hd].astype(jnp.bfloat16)
    totals = o[:, hd : hd + 1]
    for i in range(n_seg):
        r = slice(i * rows, (i + 1) * rows)
        out_ref[i, :rows, :] = mixed[r]
        out_ref[i, rows:, :] = stat_rows(hi[r], lo[r], totals[r])


def suffix_kernel(c, heads, len_ref, q_ref, k_ref, v_ref, out_ref):
    forks, slots, hd = k_ref.shape
    rows = q_ref.shape[0] // forks
    his, los, tots = [], [], []
    for f in range(forks):
        q = q_ref[f * rows : (f + 1) * rows, :]
        s = dot(q, k_ref[f], 1, 1)
        step = lax.broadcasted_iota(jnp.int32, (rows, slots), 0) // heads
        slot = lax.broadcasted_iota(jnp.int32, (rows, slots), 1)
        s = jnp.where(slot < len_ref[f] + step + 1, s, NEG)
        hi, lo, shift = shift_of(jnp.max(s, axis=1, keepdims=True))
        p = jnp.exp2((s - shift) * c)
        out_ref[f * rows : (f + 1) * rows, :] = dot(
            p.astype(jnp.bfloat16), v_ref[f], 1, 0
        ).astype(jnp.bfloat16)
        his.append(hi)
        los.append(lo)
        tots.append(jnp.sum(p, axis=1, keepdims=True))
    cat = functools.partial(jnp.concatenate, axis=0)
    out_ref[forks * rows :, :] = stat_rows(cat(his), cat(los), cat(tots))


def combine_kernel(c, got_ref, own_ref, out_ref):
    n = got_ref.shape[0]
    rows = own_ref.shape[0] - STATS
    f = jnp.float32
    m = got_ref[:, rows, :].astype(f) + got_ref[:, rows + 1, :].astype(f)
    t = got_ref[:, rows + 2, :].astype(f) + got_ref[:, rows + 3, :].astype(f)
    own = own_ref[rows:, :].astype(f)
    m_own = own[0:1] + own[1:2]
    t_own = own[2:3] + own[3:4]
    top = jnp.maximum(jnp.max(m, axis=0, keepdims=True), m_own)
    a = jnp.exp2((m - top) * c)
    a_own = jnp.exp2((m_own - top) * c)
    whole = jnp.sum(a * t, axis=0, keepdims=True) + a_own * t_own
    inv = 1.0 / whole
    table = jnp.concatenate(
        [a * inv, a_own * inv, jnp.zeros((128 - n - 1, 128), f)], axis=0
    )
    coef = jnp.transpose(table)
    acc = own_ref[:rows, :].astype(f) * coef[:rows, n : n + 1]
    for i in range(n):
        acc = acc + got_ref[i, :rows, :].astype(f) * coef[:rows, i : i + 1]
    att = acc.astype(jnp.bfloat16)
    for i in range(out_ref.shape[0]):
        out_ref[i] = att


def project_kernel(heads, core_ref, own_ref, other_ref, w_ref, out_ref, x_ref):
    n, rows, hd = own_ref.shape
    core = core_ref[0]
    x4 = x_ref.reshape(n, 2, rows, hd)
    x4[:, core] = own_ref[...].astype(jnp.float32)
    x4[:, 1 - core] = other_ref[...].astype(jnp.float32)
    total = n * 2 * rows // heads
    acc = jnp.zeros((total, w_ref.shape[1]), jnp.float32)
    for h in range(0, heads, 2):
        pair = [
            x_ref[pl.ds(h + j, total, stride=heads), :].astype(jnp.bfloat16) for j in range(2)
        ]
        lhs = jnp.concatenate(pair, axis=1)
        acc = acc + dot(lhs, w_ref[h * hd : (h + 2) * hd, :], 1, 0)
    out_ref[...] = acc.astype(jnp.bfloat16).reshape(out_ref.shape)


def whole(n):
    return [pl.BlockSpec(memory_space=VMEM)] * n


def shards(q, pk, pv, sk, sv, lengths, w):
    forks, steps, heads, hd = q.shape
    rows = forks * steps * heads
    keys = pk.shape[0]
    slots = sk.shape[1]
    c = hd**-0.5 * LOG2E
    chips = lax.axis_size(CHIPS)
    n_tp = lax.axis_size(TP)
    cols = w.shape[1]
    bf = jnp.bfloat16
    swap = [(0, 1), (1, 0)]

    q = q.reshape(rows, hd)
    every = lax.all_to_all(
        jnp.broadcast_to(q[None], (chips, rows, hd)), CHIPS, 0, 0, tiled=True
    )
    k_own, v_own = pk.reshape(keys, hd), pv.reshape(keys, hd)
    k_pair = lax.ppermute(k_own, "core", swap)
    v_pair = lax.ppermute(v_own, "core", swap)

    own = pl.pallas_call(
        functools.partial(suffix_kernel, c, heads),
        out_shape=jax.ShapeDtypeStruct((rows + STATS, hd), bf),
        in_specs=[pl.BlockSpec(memory_space=pltpu.SMEM)] + whole(3),
        out_specs=pl.BlockSpec(memory_space=VMEM),
        cost_estimate=pl.CostEstimate(
            flops=4 * rows * slots * hd, bytes_accessed=4 * forks * slots * hd, transcendentals=rows * slots
        ),
        name="suffix",
    )(lengths, q, sk.reshape(forks, slots, hd), sv.reshape(forks, slots, hd))

    seg = 2
    states = pl.pallas_call(
        functools.partial(prefix_kernel, c),
        grid=(chips // seg,),
        out_shape=jax.ShapeDtypeStruct((chips, rows + STATS, hd), bf),
        in_specs=[pl.BlockSpec((seg, rows, hd), lambda i: (i, 0, 0))] + whole(4),
        out_specs=pl.BlockSpec((seg, rows + STATS, hd), lambda i: (i, 0, 0)),
        scratch_shapes=[VMEM((2 * keys, 2 * hd), bf)],
        name="prefix",
    )(every, k_own, k_pair, v_own, v_pair)

    got = lax.all_to_all(states, CHIPS, 0, 0, tiled=True)
    att = pl.pallas_call(
        functools.partial(combine_kernel, c),
        out_shape=jax.ShapeDtypeStruct((chips, rows, hd), bf),
        in_specs=whole(2),
        out_specs=pl.BlockSpec(memory_space=VMEM),
        name="combine",
    )(got, own)

    att = lax.all_to_all(att, CHIPS, 0, 0, tiled=True)
    other = lax.ppermute(att, "core", swap)
    core = lax.axis_index("core").astype(jnp.int32).reshape(1)
    all_rows = chips * 2 * forks * steps
    product = pl.pallas_call(
        functools.partial(project_kernel, heads),
        out_shape=jax.ShapeDtypeStruct((n_tp, all_rows // n_tp, cols), bf),
        in_specs=[pl.BlockSpec(memory_space=pltpu.SMEM)] + whole(3),
        out_specs=pl.BlockSpec(memory_space=VMEM),
        scratch_shapes=[VMEM((chips * 2 * rows, hd), jnp.float32)],
        name="project",
    )(core, att, other, w)
    parts = lax.all_to_all(product, TP, 0, 0, tiled=True)
    out = parts.astype(jnp.float32).sum(axis=0).astype(bf)
    return out.reshape(all_rows // n_tp // steps, steps, cols)


def solution(mesh):
    fine = Mesh(
        mesh.devices.reshape(2, mesh.shape["ctx"] // 4, 2, 2, mesh.shape["tp"] // 2),
        CTX + TP,
    )
    return jax.shard_map(
        shards,
        mesh=fine,
        in_specs=(
            P(CTX, None, TP, None),
            P(CTX, TP, None),
            P(CTX, TP, None),
            P(CTX, None, TP, None),
            P(CTX, None, TP, None),
            P(CTX),
            P(TP, CTX),
        ),
        out_specs=P(TP, None, CTX),
        check_vma=False,
    )
```

```python
import functools

import jax
import jax.numpy as jnp
from jax import lax
from jax.experimental import pallas as pl
from jax.experimental.pallas import tpu as pltpu
from jax._src.pallas.mosaic import core as pltpu_core
from jax.sharding import Mesh
from jax.sharding import PartitionSpec as P

CTX = ("xh", "z", "core")
CHIPS = ("xh", "z")
TP = ("xl", "y")
STATS = 8
NEG = -1e30
TILE = 256
PART = 768
UNROLL = 4
LOG2E = 1.4426950408889634
VMEM = pltpu.VMEM


def dot(a, b, ca, cb):
    return lax.dot_general(
        a, b, (((ca,), (cb,)), ((), ())), preferred_element_type=jnp.float32
    )


def shift_of(scores_max):
    hi = scores_max.astype(jnp.bfloat16)
    lo = (scores_max - hi.astype(jnp.float32)).astype(jnp.bfloat16)
    return hi, lo, hi.astype(jnp.float32) + lo.astype(jnp.float32)


def stat_rows(hi, lo, totals):
    rows = hi.shape[0]
    t_hi = totals.astype(jnp.bfloat16)
    t_lo = (totals - t_hi.astype(jnp.float32)).astype(jnp.bfloat16)
    lane = lax.broadcasted_iota(jnp.int32, (rows, 128), 1)
    f = jnp.float32
    table = jnp.where(
        lane == 0,
        hi.astype(f),
        jnp.where(
            lane == 1,
            lo.astype(f),
            jnp.where(lane == 2, t_hi.astype(f), jnp.where(lane == 3, t_lo.astype(f), 0.0)),
        ),
    ).astype(jnp.bfloat16)
    if rows < 128:
        table = jnp.concatenate([table, jnp.zeros((128 - rows, 128), jnp.bfloat16)], axis=0)
    pick = (
        lax.broadcasted_iota(jnp.int32, (STATS, 128), 0)
        == lax.broadcasted_iota(jnp.int32, (STATS, 128), 1)
    ).astype(jnp.bfloat16)
    return dot(pick, table, 1, 1).astype(jnp.bfloat16)


def accumulator(mxu, rows):
    return pltpu_core.AccMemorySpace(mxu)((rows, TILE), jnp.float32)


def prefix_kernel(c, q_ref, ko_ref, kp_ref, vo_ref, vp_ref, out_ref, q2, s_o, s_p, m_ref, o_ref):
    n, rows, hd = q_ref.shape
    total = n * rows
    keys = ko_ref.shape[0]
    f, bf = jnp.float32, jnp.bfloat16
    scores, ks, vs = (s_o, s_p), (ko_ref, kp_ref), (vo_ref, vp_ref)

    scaled = q_ref[...].reshape(total, hd).astype(f) * c
    high = scaled.astype(bf)
    q2[:, :hd] = high
    q2[:, hd:] = (scaled - high.astype(f)).astype(bf)
    m_ref[...] = jnp.full(m_ref.shape, -jnp.inf, f)

    def pass_a(*accs):
        @pl.loop(0, keys // TILE // UNROLL)
        def _(outer):
            for w in range(UNROLL):
                at = pl.ds(pl.multiple_of((outer * UNROLL + w) * TILE, TILE), TILE)
                for x in range(2):
                    k = ks[x][at, :]
                    pltpu.matmul_push_rhs(
                        jnp.concatenate([k, k], axis=1), w % 2, x, transpose=True
                    )
                for r in range(total // TILE):
                    rs = slice(r * TILE, (r + 1) * TILE)
                    for x in range(2):
                        pltpu.matmul_acc_lhs(
                            accs[2 * (r % 2) + x],
                            q2[rs, :],
                            load_staged_rhs=w % 2 if r == 0 else None,
                        )
                    tops = []
                    for x in range(2):
                        s = pltpu.matmul_pop(accs[2 * (r % 2) + x])
                        scores[x][rs, at] = s
                        tops.append(jnp.maximum(s[:, :128], s[:, 128:]))
                    m_ref[rs, :] = jnp.maximum(jnp.maximum(tops[0], tops[1]), m_ref[rs, :])

    pl.run_scoped(pass_a, *[accumulator(i % 2, TILE) for i in range(4)])
    shift = shift_of(jnp.max(m_ref[...], axis=1, keepdims=True))[2]
    m_ref[...] = jnp.broadcast_to(shift, m_ref.shape)
    ones = jnp.ones((TILE, TILE - hd), bf)
    parts = PART // TILE

    def pass_b(*accs):
        for b in range(total // PART):

            @pl.loop(0, keys // TILE // UNROLL)
            def _(outer):
                for w in range(UNROLL):
                    at = pl.ds(pl.multiple_of((outer * UNROLL + w) * TILE, TILE), TILE)
                    for x in range(2):
                        pltpu.matmul_push_rhs(
                            jnp.concatenate([vs[x][at, :], ones], axis=1), w % 2, x
                        )
                    for u in range(parts):
                        rs = slice(b * PART + u * TILE, b * PART + (u + 1) * TILE)
                        m = m_ref[rs, :]
                        m = jnp.concatenate([m, m], axis=1)
                        for x in range(2):
                            p = jnp.exp2(scores[x][rs, at] - m).astype(bf)
                            pltpu.matmul_acc_lhs(
                                accs[x * parts + u], p, load_staged_rhs=w % 2 if u == 0 else None
                            )

            for u in range(parts):
                rs = slice(b * PART + u * TILE, b * PART + (u + 1) * TILE)
                o_ref[rs, :] = pltpu.matmul_pop(accs[u]) + pltpu.matmul_pop(accs[parts + u])

    pl.run_scoped(pass_b, *[accumulator(i // parts, TILE) for i in range(2 * parts)])

    lane = lax.broadcasted_iota(jnp.int32, (rows, 128), 1)
    table = jnp.zeros((rows, 128), f)
    for i in range(n):
        rs = slice(i * rows, (i + 1) * rows)
        out_ref[i, :rows, :] = o_ref[rs, :hd].astype(bf)
        t, m = o_ref[rs, hd:], m_ref[rs, :]
        hi, t_hi = m.astype(bf).astype(f), t.astype(bf).astype(f)
        for l, v in enumerate((hi, m - hi, t_hi, t - t_hi)):
            table = jnp.where(lane == STATS * i + l, v, table)
    turned = jnp.transpose(jnp.concatenate([table, jnp.zeros((128 - rows, 128), f)], axis=0))
    for i in range(n):
        out_ref[i, rows:, :] = turned[STATS * i : STATS * (i + 1)].astype(bf)


def suffix_kernel(c, heads, len_ref, q_ref, k_ref, v_ref, out_ref):
    forks, slots, hd = k_ref.shape
    rows = q_ref.shape[0] // forks
    his, los, tots = [], [], []
    for f in range(forks):
        q = q_ref[f * rows : (f + 1) * rows, :]
        s = dot(q, k_ref[f], 1, 1) * c
        step = lax.broadcasted_iota(jnp.int32, (rows, slots), 0) // heads
        slot = lax.broadcasted_iota(jnp.int32, (rows, slots), 1)
        s = jnp.where(slot < len_ref[f] + step + 1, s, NEG)
        hi, lo, shift = shift_of(jnp.max(s, axis=1, keepdims=True))
        p = jnp.exp2(s - shift)
        out_ref[f * rows : (f + 1) * rows, :] = dot(
            p.astype(jnp.bfloat16), v_ref[f], 1, 0
        ).astype(jnp.bfloat16)
        his.append(hi)
        los.append(lo)
        tots.append(jnp.sum(p, axis=1, keepdims=True))
    cat = functools.partial(jnp.concatenate, axis=0)
    out_ref[forks * rows :, :] = stat_rows(cat(his), cat(los), cat(tots))


def combine_kernel(got_ref, own_ref, out_ref):
    n = got_ref.shape[0]
    rows = own_ref.shape[0] - STATS
    f = jnp.float32
    m = got_ref[:, rows, :].astype(f) + got_ref[:, rows + 1, :].astype(f)
    t = got_ref[:, rows + 2, :].astype(f) + got_ref[:, rows + 3, :].astype(f)
    own = own_ref[rows:, :].astype(f)
    m_own = own[0:1] + own[1:2]
    t_own = own[2:3] + own[3:4]
    top = jnp.maximum(jnp.max(m, axis=0, keepdims=True), m_own)
    a = jnp.exp2(m - top)
    a_own = jnp.exp2(m_own - top)
    whole = jnp.sum(a * t, axis=0, keepdims=True) + a_own * t_own
    inv = 1.0 / whole
    table = jnp.concatenate(
        [a * inv, a_own * inv, jnp.zeros((128 - n - 1, 128), f)], axis=0
    )
    coef = jnp.transpose(table)
    acc = own_ref[:rows, :].astype(f) * coef[:rows, n : n + 1]
    for i in range(n):
        acc = acc + got_ref[i, :rows, :].astype(f) * coef[:rows, i : i + 1]
    att = acc.astype(jnp.bfloat16)
    for i in range(out_ref.shape[0]):
        out_ref[i] = att


def project_kernel(heads, steps, core_ref, own_ref, other_ref, w_ref, out_ref, x_ref):
    n, rows, hd = own_ref.shape
    core = core_ref[0]
    x4 = x_ref.reshape(n, 2, rows, hd)
    x4[:, core] = own_ref[...].astype(jnp.float32)
    x4[:, 1 - core] = other_ref[...].astype(jnp.float32)
    forks = n * 2 * rows // heads // steps
    acc = jnp.zeros((steps * forks, w_ref.shape[1]), jnp.float32)
    for h in range(0, heads, 2):
        pair = [
            jnp.concatenate(
                [
                    x_ref[pl.ds(s * heads + h + j, forks, stride=steps * heads), :]
                    for s in range(steps)
                ],
                axis=0,
            ).astype(jnp.bfloat16)
            for j in range(2)
        ]
        lhs = jnp.concatenate(pair, axis=1)
        acc = acc + dot(lhs, w_ref[h * hd : (h + 2) * hd, :], 1, 0)
    tps = out_ref.shape[0]
    mine = forks // tps
    for s in range(steps):
        block = acc[s * forks : (s + 1) * forks].astype(jnp.bfloat16)
        out_ref[:, s] = block.reshape(tps, mine, -1)


def sum_kernel(parts_ref, out_ref):
    out_ref[...] = jnp.sum(parts_ref[...].astype(jnp.float32), axis=0).astype(jnp.bfloat16)


def whole(n):
    return [pl.BlockSpec(memory_space=VMEM)] * n


def shards(q, pk, pv, sk, sv, lengths, w):
    forks, steps, heads, hd = q.shape
    rows = forks * steps * heads
    keys = pk.shape[0]
    slots = sk.shape[1]
    c = hd**-0.5 * LOG2E
    chips = lax.axis_size(CHIPS)
    n_tp = lax.axis_size(TP)
    cols = w.shape[1]
    bf = jnp.bfloat16
    swap = [(0, 1), (1, 0)]

    q = q.reshape(rows, hd)
    every = lax.all_to_all(
        jnp.broadcast_to(q[None], (chips, rows, hd)), CHIPS, 0, 0, tiled=True
    )
    k_own, v_own = pk.reshape(keys, hd), pv.reshape(keys, hd)
    k_pair = lax.ppermute(k_own, "core", swap)
    v_pair = lax.ppermute(v_own, "core", swap)

    own = pl.pallas_call(
        functools.partial(suffix_kernel, c, heads),
        out_shape=jax.ShapeDtypeStruct((rows + STATS, hd), bf),
        in_specs=[pl.BlockSpec(memory_space=pltpu.SMEM)] + whole(3),
        out_specs=pl.BlockSpec(memory_space=VMEM),
        cost_estimate=pl.CostEstimate(
            flops=4 * rows * slots * hd, bytes_accessed=4 * forks * slots * hd, transcendentals=rows * slots
        ),
        compiler_params=pltpu.CompilerParams(vmem_limit_bytes=4 * 2**20),
        name="suffix",
    )(lengths, q, sk.reshape(forks, slots, hd), sv.reshape(forks, slots, hd))

    total = chips * rows
    f = jnp.float32
    states = pl.pallas_call(
        functools.partial(prefix_kernel, c),
        out_shape=jax.ShapeDtypeStruct((chips, rows + STATS, hd), bf),
        in_specs=whole(5),
        out_specs=pl.BlockSpec(memory_space=VMEM),
        scratch_shapes=[
            VMEM((total, TILE), bf),
            VMEM((total, keys), f),
            VMEM((total, keys), f),
            VMEM((total, 128), f),
            VMEM((total, TILE), f),
        ],
        compiler_params=pltpu.CompilerParams(vmem_limit_bytes=36 * 2**20),
        name="prefix",
    )(every, k_own, k_pair, v_own, v_pair)

    got = lax.all_to_all(states, CHIPS, 0, 0, tiled=True)
    att = pl.pallas_call(
        combine_kernel,
        out_shape=jax.ShapeDtypeStruct((chips, rows, hd), bf),
        in_specs=whole(2),
        out_specs=pl.BlockSpec(memory_space=VMEM),
        compiler_params=pltpu.CompilerParams(vmem_limit_bytes=4 * 2**20),
        name="combine",
    )(got, own)

    att = lax.all_to_all(att, CHIPS, 0, 0, tiled=True)
    other = lax.ppermute(att, "core", swap)
    core = lax.axis_index("core").astype(jnp.int32).reshape(1)
    mine = chips * 2 * forks // n_tp
    product = pl.pallas_call(
        functools.partial(project_kernel, heads, steps),
        out_shape=jax.ShapeDtypeStruct((n_tp, steps, mine, cols), bf),
        in_specs=[pl.BlockSpec(memory_space=pltpu.SMEM)] + whole(3),
        out_specs=pl.BlockSpec(memory_space=VMEM),
        scratch_shapes=[VMEM((chips * 2 * rows, hd), jnp.float32)],
        compiler_params=pltpu.CompilerParams(vmem_limit_bytes=10 * 2**20),
        name="project",
    )(core, att, other, w)
    parts = lax.all_to_all(product, TP, 0, 0, tiled=True)
    out = pl.pallas_call(
        sum_kernel,
        out_shape=jax.ShapeDtypeStruct((steps, mine, cols), bf),
        in_specs=whole(1),
        out_specs=pl.BlockSpec(memory_space=VMEM),
        compiler_params=pltpu.CompilerParams(vmem_limit_bytes=2 * 2**20),
        name="total",
    )(parts)
    return jnp.swapaxes(out, 0, 1)


def solution(mesh):
    fine = Mesh(
        mesh.devices.reshape(2, mesh.shape["ctx"] // 4, 2, 2, mesh.shape["tp"] // 2),
        CTX + TP,
    )
    return jax.shard_map(
        shards,
        mesh=fine,
        in_specs=(
            P(CTX, None, TP, None),
            P(CTX, TP, None),
            P(CTX, TP, None),
            P(CTX, None, TP, None),
            P(CTX, None, TP, None),
            P(CTX),
            P(TP, CTX),
        ),
        out_specs=P(TP, None, CTX),
        check_vma=False,
    )
```

```python
import functools

import jax
import jax.numpy as jnp
from jax import lax
from jax.experimental import pallas as pl
from jax.experimental.pallas import tpu as pltpu
from jax._src.pallas.mosaic import core as pltpu_core
from jax.sharding import Mesh
from jax.sharding import PartitionSpec as P


CTX = ("xh", "z", "core")
CHIPS = ("xh", "z")
TP = ("xl", "y")
STATS = 8
NEG = -1e30
TILE = 256
UNROLL = 4
LOG2E = 1.4426950408889634
VMEM = pltpu.VMEM


def dot(a, b, ca, cb):
    return lax.dot_general(
        a, b, (((ca,), (cb,)), ((), ())), preferred_element_type=jnp.float32
    )


def shift_of(scores_max):
    hi = scores_max.astype(jnp.bfloat16)
    lo = (scores_max - hi.astype(jnp.float32)).astype(jnp.bfloat16)
    return hi, lo, hi.astype(jnp.float32) + lo.astype(jnp.float32)


def stat_rows(hi, lo, totals):
    rows = hi.shape[0]
    t_hi = totals.astype(jnp.bfloat16)
    t_lo = (totals - t_hi.astype(jnp.float32)).astype(jnp.bfloat16)
    lane = lax.broadcasted_iota(jnp.int32, (rows, 128), 1)
    f = jnp.float32
    table = jnp.where(
        lane == 0,
        hi.astype(f),
        jnp.where(
            lane == 1,
            lo.astype(f),
            jnp.where(lane == 2, t_hi.astype(f), jnp.where(lane == 3, t_lo.astype(f), 0.0)),
        ),
    ).astype(jnp.bfloat16)
    if rows < 128:
        table = jnp.concatenate([table, jnp.zeros((128 - rows, 128), jnp.bfloat16)], axis=0)
    pick = (
        lax.broadcasted_iota(jnp.int32, (STATS, 128), 0)
        == lax.broadcasted_iota(jnp.int32, (STATS, 128), 1)
    ).astype(jnp.bfloat16)
    return dot(pick, table, 1, 1).astype(jnp.bfloat16)


def accumulator(mxu, rows):
    return pltpu_core.AccMemorySpace(mxu)((rows, TILE), jnp.float32)


def scaled_queries(c, q_ref, q2):
    n, rows, hd = q_ref.shape
    f, bf = jnp.float32, jnp.bfloat16
    scaled = q_ref[...].reshape(n * rows, hd).astype(f) * c
    high = scaled.astype(bf)
    q2[:, :hd] = high
    q2[:, hd:] = (scaled - high.astype(f)).astype(bf)


def score_pass(q2, ks, scores, m_ref):
    keys = ks[0].shape[0]
    total = q2.shape[0]

    def body(*accs):
        @pl.loop(0, keys // TILE // UNROLL)
        def _(outer):
            for w in range(UNROLL):
                at = pl.ds(pl.multiple_of((outer * UNROLL + w) * TILE, TILE), TILE)
                for x in range(2):
                    k = ks[x][at, :]
                    pltpu.matmul_push_rhs(
                        jnp.concatenate([k, k], axis=1), w % 2, x, transpose=True
                    )
                for r in range(total // TILE):
                    rs = slice(r * TILE, (r + 1) * TILE)
                    for x in range(2):
                        pltpu.matmul_acc_lhs(
                            accs[2 * (r % 2) + x],
                            q2[rs, :],
                            load_staged_rhs=w % 2 if r == 0 else None,
                        )
                    tops = []
                    for x in range(2):
                        s = pltpu.matmul_pop(accs[2 * (r % 2) + x])
                        scores[x][rs, at] = s
                        tops.append(jnp.maximum(s[:, :128], s[:, 128:]))
                    m_ref[rs, :] = jnp.maximum(jnp.maximum(tops[0], tops[1]), m_ref[rs, :])

    pl.run_scoped(body, *[accumulator(i % 2, TILE) for i in range(4)])
    shift = shift_of(jnp.max(m_ref[...], axis=1, keepdims=True))[2]
    m_ref[...] = jnp.broadcast_to(shift, m_ref.shape)


def mix_pass(vs, scores, m_ref, o_ref):
    keys, hd = vs[0].shape
    total = m_ref.shape[0]
    parts = total // TILE
    bf = jnp.bfloat16
    ones = jnp.ones((TILE, TILE - hd), bf)

    def body(*accs):
        @pl.loop(0, keys // TILE // UNROLL)
        def _(outer):
            for w in range(UNROLL):
                at = pl.ds(pl.multiple_of((outer * UNROLL + w) * TILE, TILE), TILE)
                for x in range(2):
                    pltpu.matmul_push_rhs(
                        jnp.concatenate([vs[x][at, :], ones], axis=1), w % 2, x
                    )
                for u in range(parts):
                    rs = slice(u * TILE, (u + 1) * TILE)
                    m = m_ref[rs, :]
                    m = jnp.concatenate([m, m], axis=1)
                    for x in range(2):
                        p = jnp.exp2(scores[x][rs, at] - m).astype(bf)
                        pltpu.matmul_acc_lhs(
                            accs[x * parts + u], p, load_staged_rhs=w % 2 if u == 0 else None
                        )

        for u in range(parts):
            rs = slice(u * TILE, (u + 1) * TILE)
            o_ref[rs, :] = pltpu.matmul_pop(accs[u]) + pltpu.matmul_pop(accs[parts + u])

    pl.run_scoped(body, *[accumulator(i // parts, TILE) for i in range(2 * parts)])


def near_kernel(
    c, q_ref, ko_ref, kp_ref, vo_ref, vp_ref, o_ref, m_ref, q2, s_o, s_p, k_buf, v_buf, sems
):
    get_k = pltpu.make_async_copy(ko_ref, k_buf, sems.at[0])
    get_v = pltpu.make_async_copy(vo_ref, v_buf, sems.at[1])
    get_k.start()
    get_v.start()
    scaled_queries(c, q_ref, q2)
    m_ref[...] = jnp.full(m_ref.shape, -jnp.inf, jnp.float32)
    get_k.wait()
    score_pass(q2, (k_buf, kp_ref), (s_o, s_p), m_ref)
    get_v.wait()
    mix_pass((v_buf, vp_ref), (s_o, s_p), m_ref, o_ref)


def far_kernel(
    c, q_ref, ko_ref, kp_ref, vo_ref, vp_ref, o1_ref, m1_ref, out_ref, q2, s_o, s_p, m_ref, o_ref
):
    n, rows, hd = q_ref.shape
    f, bf = jnp.float32, jnp.bfloat16
    scaled_queries(c, q_ref, q2)
    m_ref[...] = m1_ref[...]
    score_pass(q2, (ko_ref, kp_ref), (s_o, s_p), m_ref)
    mix_pass((vo_ref, vp_ref), (s_o, s_p), m_ref, o_ref)

    lane = lax.broadcasted_iota(jnp.int32, (rows, 128), 1)
    table = jnp.zeros((rows, 128), f)
    for i in range(n):
        rs = slice(i * rows, (i + 1) * rows)
        m = m_ref[rs, :]
        a = jnp.exp2(m1_ref[rs, :] - m)
        out_ref[i, :rows, :] = (o_ref[rs, :hd] + a * o1_ref[rs, :hd]).astype(bf)
        t = o_ref[rs, hd:] + a * o1_ref[rs, hd:]
        hi, t_hi = m.astype(bf).astype(f), t.astype(bf).astype(f)
        for l, v in enumerate((hi, m - hi, t_hi, t - t_hi)):
            table = jnp.where(lane == STATS * i + l, v, table)
    turned = jnp.transpose(jnp.concatenate([table, jnp.zeros((128 - rows, 128), f)], axis=0))
    for i in range(n):
        out_ref[i, rows:, :] = turned[STATS * i : STATS * (i + 1)].astype(bf)


def suffix_kernel(c, heads, len_ref, q_ref, k_ref, v_ref, out_ref):
    forks, slots, _ = k_ref.shape
    rows = q_ref.shape[0] // forks
    his, los, tots = [], [], []
    for f in range(forks):
        q = q_ref[f * rows : (f + 1) * rows, :]
        s = dot(q, k_ref[f], 1, 1) * c
        step = lax.broadcasted_iota(jnp.int32, (rows, slots), 0) // heads
        slot = lax.broadcasted_iota(jnp.int32, (rows, slots), 1)
        s = jnp.where(slot < len_ref[f] + step + 1, s, NEG)
        hi, lo, shift = shift_of(jnp.max(s, axis=1, keepdims=True))
        p = jnp.exp2(s - shift)
        out_ref[f * rows : (f + 1) * rows, :] = dot(
            p.astype(jnp.bfloat16), v_ref[f], 1, 0
        ).astype(jnp.bfloat16)
        his.append(hi)
        los.append(lo)
        tots.append(jnp.sum(p, axis=1, keepdims=True))
    cat = functools.partial(jnp.concatenate, axis=0)
    out_ref[forks * rows :, :] = stat_rows(cat(his), cat(los), cat(tots))


def combine_kernel(got_ref, own_ref, out_ref):
    n = got_ref.shape[0]
    rows = own_ref.shape[0] - STATS
    f = jnp.float32
    m = got_ref[:, rows, :].astype(f) + got_ref[:, rows + 1, :].astype(f)
    t = got_ref[:, rows + 2, :].astype(f) + got_ref[:, rows + 3, :].astype(f)
    own = own_ref[rows:, :].astype(f)
    m_own = own[0:1] + own[1:2]
    t_own = own[2:3] + own[3:4]
    top = jnp.maximum(jnp.max(m, axis=0, keepdims=True), m_own)
    a = jnp.exp2(m - top)
    a_own = jnp.exp2(m_own - top)
    whole = jnp.sum(a * t, axis=0, keepdims=True) + a_own * t_own
    inv = 1.0 / whole
    table = jnp.concatenate(
        [a * inv, a_own * inv, jnp.zeros((128 - n - 1, 128), f)], axis=0
    )
    coef = jnp.transpose(table)
    acc = own_ref[:rows, :].astype(f) * coef[:rows, n : n + 1]
    for i in range(n):
        acc = acc + got_ref[i, :rows, :].astype(f) * coef[:rows, i : i + 1]
    att = acc.astype(jnp.bfloat16)
    for i in range(out_ref.shape[0]):
        out_ref[i] = att


def project_kernel(heads, steps, core_ref, own_ref, other_ref, w_ref, out_ref, x_ref):
    n, rows, hd = own_ref.shape
    core = core_ref[0]
    x4 = x_ref.reshape(n, 2, rows, hd)
    x4[:, core] = own_ref[...].astype(jnp.float32)
    x4[:, 1 - core] = other_ref[...].astype(jnp.float32)
    forks = n * 2 * rows // heads // steps
    acc = jnp.zeros((steps * forks, w_ref.shape[1]), jnp.float32)
    for h in range(0, heads, 2):
        pair = [
            jnp.concatenate(
                [
                    x_ref[pl.ds(s * heads + h + j, forks, stride=steps * heads), :]
                    for s in range(steps)
                ],
                axis=0,
            ).astype(jnp.bfloat16)
            for j in range(2)
        ]
        lhs = jnp.concatenate(pair, axis=1)
        acc = acc + dot(lhs, w_ref[h * hd : (h + 2) * hd, :], 1, 0)
    tps = out_ref.shape[0]
    mine = forks // tps
    for s in range(steps):
        block = acc[s * forks : (s + 1) * forks].astype(jnp.bfloat16)
        out_ref[:, s] = block.reshape(tps, mine, -1)


def sum_kernel(parts_ref, out_ref):
    out_ref[...] = jnp.sum(parts_ref[...].astype(jnp.float32), axis=0).astype(jnp.bfloat16)


def whole(n):
    return [pl.BlockSpec(memory_space=VMEM)] * n


def body(q, pk, pv, sk, sv, lengths, w):
    forks, steps, heads, hd = q.shape
    rows = forks * steps * heads
    keys = pk.shape[0]
    slots = sk.shape[1]
    c = hd**-0.5 * LOG2E
    chips = lax.axis_size(CHIPS)
    n_tp = lax.axis_size(TP)
    cols = w.shape[1]
    bf = jnp.bfloat16
    swap = [(0, 1), (1, 0)]

    k_own, v_own = pk.reshape(keys, hd), pv.reshape(keys, hd)
    k_far = lax.ppermute(k_own, "xh", swap)
    v_far = lax.ppermute(v_own, "xh", swap)
    k_pair = lax.ppermute(k_own, "core", swap)
    v_pair = lax.ppermute(v_own, "core", swap)
    q = q.reshape(rows, hd)
    ring = lax.axis_size("z")
    every = lax.all_to_all(
        jnp.broadcast_to(q[None], (ring, rows, hd)), "z", 0, 0, tiled=True
    )
    every, k_far = lax.optimization_barrier((every, k_far))
    k_far_pair = lax.ppermute(k_far, "core", swap)
    every, k_far_pair = lax.optimization_barrier((every, k_far_pair))

    own = pl.pallas_call(
        functools.partial(suffix_kernel, c, heads),
        out_shape=jax.ShapeDtypeStruct((rows + STATS, hd), bf),
        in_specs=[pl.BlockSpec(memory_space=pltpu.SMEM)] + whole(3),
        out_specs=pl.BlockSpec(memory_space=VMEM),
        cost_estimate=pl.CostEstimate(
            flops=4 * rows * slots * hd, bytes_accessed=4 * forks * slots * hd, transcendentals=rows * slots
        ),
        compiler_params=pltpu.CompilerParams(vmem_limit_bytes=4 * 2**20),
        name="suffix",
    )(lengths, q, sk.reshape(forks, slots, hd), sv.reshape(forks, slots, hd))

    total = ring * rows
    f = jnp.float32
    near = pl.pallas_call(
        functools.partial(near_kernel, c),
        out_shape=[
            jax.ShapeDtypeStruct((total, TILE), f),
            jax.ShapeDtypeStruct((total, 128), f),
        ],
        in_specs=[
            pl.BlockSpec(memory_space=VMEM),
            pl.BlockSpec(memory_space=pltpu.HBM),
            pl.BlockSpec(memory_space=VMEM),
            pl.BlockSpec(memory_space=pltpu.HBM),
            pl.BlockSpec(memory_space=VMEM),
        ],
        out_specs=whole(2),
        scratch_shapes=[
            VMEM((total, TILE), bf),
            VMEM((total, keys), f),
            VMEM((total, keys), f),
            VMEM((keys, hd), bf),
            VMEM((keys, hd), bf),
            pltpu.SemaphoreType.DMA((2,)),
        ],
        compiler_params=pltpu.CompilerParams(vmem_limit_bytes=20 * 2**20),
        cost_estimate=pl.CostEstimate(
            flops=8 * total * keys * hd, bytes_accessed=8 * keys * hd, transcendentals=2 * total * keys
        ),
        name="near",
    )(every, k_own, k_pair, v_own, v_pair)
    o1, m1, v_far = lax.optimization_barrier((*near, v_far))
    v_far_pair = lax.ppermute(v_far, "core", swap)
    states = pl.pallas_call(
        functools.partial(far_kernel, c),
        out_shape=jax.ShapeDtypeStruct((ring, rows + STATS, hd), bf),
        in_specs=whole(7),
        out_specs=pl.BlockSpec(memory_space=VMEM),
        scratch_shapes=[
            VMEM((total, TILE), bf),
            VMEM((total, keys), f),
            VMEM((total, keys), f),
            VMEM((total, 128), f),
            VMEM((total, TILE), f),
        ],
        compiler_params=pltpu.CompilerParams(vmem_limit_bytes=22 * 2**20),
        cost_estimate=pl.CostEstimate(
            flops=8 * total * keys * hd, bytes_accessed=8 * keys * hd, transcendentals=2 * total * keys
        ),
        name="far",
    )(every, k_far, k_far_pair, v_far, v_far_pair, o1, m1)

    got = lax.all_to_all(states, "z", 0, 0, tiled=True)
    att = pl.pallas_call(
        combine_kernel,
        out_shape=jax.ShapeDtypeStruct((chips, rows, hd), bf),
        in_specs=whole(2),
        out_specs=pl.BlockSpec(memory_space=VMEM),
        compiler_params=pltpu.CompilerParams(vmem_limit_bytes=4 * 2**20),
        name="combine",
    )(got, own)

    att = lax.all_to_all(att, CHIPS, 0, 0, tiled=True)
    other = lax.ppermute(att, "core", swap)
    core = lax.axis_index("core").astype(jnp.int32).reshape(1)
    mine = chips * 2 * forks // n_tp
    product = pl.pallas_call(
        functools.partial(project_kernel, heads, steps),
        out_shape=jax.ShapeDtypeStruct((n_tp, steps, mine, cols), bf),
        in_specs=[pl.BlockSpec(memory_space=pltpu.SMEM)] + whole(3),
        out_specs=pl.BlockSpec(memory_space=VMEM),
        scratch_shapes=[VMEM((chips * 2 * rows, hd), jnp.float32)],
        compiler_params=pltpu.CompilerParams(vmem_limit_bytes=10 * 2**20),
        name="project",
    )(core, att, other, w)
    parts = lax.all_to_all(product, TP, 0, 0, tiled=True)
    out = pl.pallas_call(
        sum_kernel,
        out_shape=jax.ShapeDtypeStruct((steps, mine, cols), bf),
        in_specs=whole(1),
        out_specs=pl.BlockSpec(memory_space=VMEM),
        compiler_params=pltpu.CompilerParams(vmem_limit_bytes=2 * 2**20),
        name="total",
    )(parts)
    return jnp.swapaxes(out, 0, 1)


def solution(mesh):
    fine = Mesh(
        mesh.devices.reshape(2, mesh.shape["ctx"] // 4, 2, 2, mesh.shape["tp"] // 2),
        CTX + TP,
    )
    return jax.shard_map(
        body,
        mesh=fine,
        in_specs=(
            P(CTX, None, TP, None),
            P(CTX, TP, None),
            P(CTX, TP, None),
            P(CTX, None, TP, None),
            P(CTX, None, TP, None),
            P(CTX),
            P(TP, CTX),
        ),
        out_specs=P(TP, None, CTX),
        check_vma=False,
    )
```

```python
import functools

import jax
import jax.numpy as jnp
from jax import lax
from jax.experimental import pallas as pl
from jax.experimental.pallas import tpu as pltpu
from jax._src.pallas.mosaic import core as pltpu_core
from jax.sharding import Mesh
from jax.sharding import PartitionSpec as P


CTX = ("xh", "z", "core")
CHIPS = ("xh", "z")
TP = ("xl", "y")
STATS = 8
NEG = -1e30
TILE = 256
UNROLL = 4
LOG2E = 1.4426950408889634
VMEM = pltpu.VMEM


def dot(a, b, ca, cb):
    return lax.dot_general(
        a, b, (((ca,), (cb,)), ((), ())), preferred_element_type=jnp.float32
    )


def shift_of(scores_max):
    hi = scores_max.astype(jnp.bfloat16)
    lo = (scores_max - hi.astype(jnp.float32)).astype(jnp.bfloat16)
    return hi, lo, hi.astype(jnp.float32) + lo.astype(jnp.float32)


def stat_rows(hi, lo, totals):
    rows = hi.shape[0]
    t_hi = totals.astype(jnp.bfloat16)
    t_lo = (totals - t_hi.astype(jnp.float32)).astype(jnp.bfloat16)
    lane = lax.broadcasted_iota(jnp.int32, (rows, 128), 1)
    f = jnp.float32
    table = jnp.where(
        lane == 0,
        hi.astype(f),
        jnp.where(
            lane == 1,
            lo.astype(f),
            jnp.where(lane == 2, t_hi.astype(f), jnp.where(lane == 3, t_lo.astype(f), 0.0)),
        ),
    ).astype(jnp.bfloat16)
    if rows < 128:
        table = jnp.concatenate([table, jnp.zeros((128 - rows, 128), jnp.bfloat16)], axis=0)
    pick = (
        lax.broadcasted_iota(jnp.int32, (STATS, 128), 0)
        == lax.broadcasted_iota(jnp.int32, (STATS, 128), 1)
    ).astype(jnp.bfloat16)
    return dot(pick, table, 1, 1).astype(jnp.bfloat16)


def accumulator(mxu, rows):
    return pltpu_core.AccMemorySpace(mxu)((rows, TILE), jnp.float32)


def scaled_queries(c, q_ref, q2):
    n, rows, hd = q_ref.shape
    f, bf = jnp.float32, jnp.bfloat16
    scaled = q_ref[...].reshape(n * rows, hd).astype(f) * c
    high = scaled.astype(bf)
    q2[:, :hd] = high
    q2[:, hd:] = (scaled - high.astype(f)).astype(bf)


def score_pass(q2, ks, scores, m_ref):
    keys = ks[0].shape[0]
    total = q2.shape[0]

    def body(*accs):
        @pl.loop(0, keys // TILE // UNROLL)
        def _(outer):
            for w in range(UNROLL):
                at = pl.ds(pl.multiple_of((outer * UNROLL + w) * TILE, TILE), TILE)
                for x in range(2):
                    k = ks[x][at, :]
                    pltpu.matmul_push_rhs(
                        jnp.concatenate([k, k], axis=1), w % 2, x, transpose=True
                    )
                for r in range(total // TILE):
                    rs = slice(r * TILE, (r + 1) * TILE)
                    for x in range(2):
                        pltpu.matmul_acc_lhs(
                            accs[2 * (r % 2) + x],
                            q2[rs, :],
                            load_staged_rhs=w % 2 if r == 0 else None,
                        )
                    tops = []
                    for x in range(2):
                        s = pltpu.matmul_pop(accs[2 * (r % 2) + x])
                        scores[x][rs, at] = s
                        tops.append(jnp.maximum(s[:, :128], s[:, 128:]))
                    m_ref[rs, :] = jnp.maximum(jnp.maximum(tops[0], tops[1]), m_ref[rs, :])

    pl.run_scoped(body, *[accumulator(i % 2, TILE) for i in range(4)])
    shift = shift_of(jnp.max(m_ref[...], axis=1, keepdims=True))[2]
    m_ref[...] = jnp.broadcast_to(shift, m_ref.shape)


def mix_pass(vs, scores, m_ref, o_ref):
    keys, hd = vs[0].shape
    total = m_ref.shape[0]
    parts = total // TILE
    bf = jnp.bfloat16
    ones = jnp.ones((TILE, TILE - hd), bf)

    def body(*accs):
        @pl.loop(0, keys // TILE // UNROLL)
        def _(outer):
            for w in range(UNROLL):
                at = pl.ds(pl.multiple_of((outer * UNROLL + w) * TILE, TILE), TILE)
                for x in range(2):
                    pltpu.matmul_push_rhs(
                        jnp.concatenate([vs[x][at, :], ones], axis=1), w % 2, x
                    )
                for u in range(parts):
                    rs = slice(u * TILE, (u + 1) * TILE)
                    m = m_ref[rs, :]
                    m = jnp.concatenate([m, m], axis=1)
                    for x in range(2):
                        p = jnp.exp2(scores[x][rs, at] - m).astype(bf)
                        pltpu.matmul_acc_lhs(
                            accs[x * parts + u], p, load_staged_rhs=w % 2 if u == 0 else None
                        )

        for u in range(parts):
            rs = slice(u * TILE, (u + 1) * TILE)
            o_ref[rs, :] = pltpu.matmul_pop(accs[u]) + pltpu.matmul_pop(accs[parts + u])

    pl.run_scoped(body, *[accumulator(i // parts, TILE) for i in range(2 * parts)])


def near_kernel(c, q_ref, ko_ref, kp_ref, vo_ref, vp_ref, o_ref, m_ref, q2, s_o, s_p):
    scaled_queries(c, q_ref, q2)
    m_ref[...] = jnp.full(m_ref.shape, -jnp.inf, jnp.float32)
    score_pass(q2, (ko_ref, kp_ref), (s_o, s_p), m_ref)
    mix_pass((vo_ref, vp_ref), (s_o, s_p), m_ref, o_ref)


def halves(ref):
    half = ref.shape[0] // 2
    return ref.at[:half], ref.at[half:]


def next_kernel(c, q_ref, k_ref, v_ref, o1_ref, m1_ref, o_ref, m_ref, q2, s_o, s_p):
    scaled_queries(c, q_ref, q2)
    m_ref[...] = m1_ref[...]
    score_pass(q2, halves(k_ref), (s_o, s_p), m_ref)
    mix_pass(halves(v_ref), (s_o, s_p), m_ref, o_ref)
    a = jnp.exp2(m1_ref[...] - m_ref[...])
    o_ref[...] = o_ref[...] + jnp.concatenate([a, a], axis=1) * o1_ref[...]


def far_kernel(
    c, q_ref, k_ref, v_ref, o1_ref, m1_ref, out_ref, q2, s_o, s_p, m_ref, o_ref
):
    n, rows, hd = q_ref.shape
    f, bf = jnp.float32, jnp.bfloat16
    scaled_queries(c, q_ref, q2)
    m_ref[...] = m1_ref[...]
    score_pass(q2, halves(k_ref), (s_o, s_p), m_ref)
    mix_pass(halves(v_ref), (s_o, s_p), m_ref, o_ref)

    lane = lax.broadcasted_iota(jnp.int32, (rows, 128), 1)
    table = jnp.zeros((rows, 128), f)
    for i in range(n):
        rs = slice(i * rows, (i + 1) * rows)
        m = m_ref[rs, :]
        a = jnp.exp2(m1_ref[rs, :] - m)
        out_ref[i, :rows, :] = (o_ref[rs, :hd] + a * o1_ref[rs, :hd]).astype(bf)
        t = o_ref[rs, hd:] + a * o1_ref[rs, hd:]
        hi, t_hi = m.astype(bf).astype(f), t.astype(bf).astype(f)
        for l, v in enumerate((hi, m - hi, t_hi, t - t_hi)):
            table = jnp.where(lane == STATS * i + l, v, table)
    turned = jnp.transpose(jnp.concatenate([table, jnp.zeros((128 - rows, 128), f)], axis=0))
    for i in range(n):
        out_ref[i, rows:, :] = turned[STATS * i : STATS * (i + 1)].astype(bf)


def suffix_kernel(
    c, heads, len_ref, q_ref, k_ref, v_ref, pk_ref, pv_ref, out_ref, k_out, v_out, sems
):
    get_k = pltpu.make_async_copy(pk_ref, k_out, sems.at[0])
    get_v = pltpu.make_async_copy(pv_ref, v_out, sems.at[1])
    get_k.start()
    get_v.start()
    forks, slots, _ = k_ref.shape
    rows = q_ref.shape[0] // forks
    his, los, tots = [], [], []
    for f in range(forks):
        q = q_ref[f * rows : (f + 1) * rows, :]
        s = dot(q, k_ref[f], 1, 1) * c
        step = lax.broadcasted_iota(jnp.int32, (rows, slots), 0) // heads
        slot = lax.broadcasted_iota(jnp.int32, (rows, slots), 1)
        s = jnp.where(slot < len_ref[f] + step + 1, s, NEG)
        hi, lo, shift = shift_of(jnp.max(s, axis=1, keepdims=True))
        p = jnp.exp2(s - shift)
        out_ref[f * rows : (f + 1) * rows, :] = dot(
            p.astype(jnp.bfloat16), v_ref[f], 1, 0
        ).astype(jnp.bfloat16)
        his.append(hi)
        los.append(lo)
        tots.append(jnp.sum(p, axis=1, keepdims=True))
    cat = functools.partial(jnp.concatenate, axis=0)
    out_ref[forks * rows :, :] = stat_rows(cat(his), cat(los), cat(tots))
    get_k.wait()
    get_v.wait()


def combine_kernel(got_ref, own_ref, out_ref):
    n = got_ref.shape[0]
    rows = own_ref.shape[0] - STATS
    f = jnp.float32
    m = got_ref[:, rows, :].astype(f) + got_ref[:, rows + 1, :].astype(f)
    t = got_ref[:, rows + 2, :].astype(f) + got_ref[:, rows + 3, :].astype(f)
    own = own_ref[rows:, :].astype(f)
    m_own = own[0:1] + own[1:2]
    t_own = own[2:3] + own[3:4]
    top = jnp.maximum(jnp.max(m, axis=0, keepdims=True), m_own)
    a = jnp.exp2(m - top)
    a_own = jnp.exp2(m_own - top)
    whole = jnp.sum(a * t, axis=0, keepdims=True) + a_own * t_own
    inv = 1.0 / whole
    table = jnp.concatenate(
        [a * inv, a_own * inv, jnp.zeros((128 - n - 1, 128), f)], axis=0
    )
    coef = jnp.transpose(table)
    acc = own_ref[:rows, :].astype(f) * coef[:rows, n : n + 1]
    for i in range(n):
        acc = acc + got_ref[i, :rows, :].astype(f) * coef[:rows, i : i + 1]
    att = acc.astype(jnp.bfloat16)
    for i in range(out_ref.shape[0]):
        out_ref[i] = att


def project_kernel(heads, steps, core_ref, own_ref, other_ref, w_ref, out_ref, x_ref):
    n, rows, hd = own_ref.shape
    core = core_ref[0]
    x4 = x_ref.reshape(n, 2, rows, hd)
    x4[:, core] = own_ref[...].astype(jnp.float32)
    x4[:, 1 - core] = other_ref[...].astype(jnp.float32)
    forks = n * 2 * rows // heads // steps
    acc = jnp.zeros((steps * forks, w_ref.shape[1]), jnp.float32)
    for h in range(0, heads, 2):
        pair = [
            jnp.concatenate(
                [
                    x_ref[pl.ds(s * heads + h + j, forks, stride=steps * heads), :]
                    for s in range(steps)
                ],
                axis=0,
            ).astype(jnp.bfloat16)
            for j in range(2)
        ]
        lhs = jnp.concatenate(pair, axis=1)
        acc = acc + dot(lhs, w_ref[h * hd : (h + 2) * hd, :], 1, 0)
    tps = out_ref.shape[0]
    mine = forks // tps
    for s in range(steps):
        block = acc[s * forks : (s + 1) * forks].astype(jnp.bfloat16)
        out_ref[:, s] = block.reshape(tps, mine, -1)


def sum_kernel(parts_ref, out_ref):
    out_ref[...] = jnp.sum(parts_ref[...].astype(jnp.float32), axis=0).astype(jnp.bfloat16)


def whole(n):
    return [pl.BlockSpec(memory_space=VMEM)] * n


def body(q, pk, pv, sk, sv, lengths, w):
    forks, steps, heads, hd = q.shape
    rows = forks * steps * heads
    keys = pk.shape[0]
    slots = sk.shape[1]
    c = hd**-0.5 * LOG2E
    chips = lax.axis_size(CHIPS)
    n_tp = lax.axis_size(TP)
    cols = w.shape[1]
    bf = jnp.bfloat16
    swap = [(0, 1), (1, 0)]

    k_own, v_own = pk.reshape(keys, hd), pv.reshape(keys, hd)
    k_far = lax.ppermute(k_own, "xh", swap)
    v_far = lax.ppermute(v_own, "xh", swap)
    k_pair = lax.ppermute(k_own, "core", swap)
    v_pair = lax.ppermute(v_own, "core", swap)
    q = q.reshape(rows, hd)
    ring = lax.axis_size("z")
    every = lax.all_to_all(
        jnp.broadcast_to(q[None], (ring, rows, hd)), "z", 0, 0, tiled=True
    )
    hbm = pl.BlockSpec(memory_space=pltpu.HBM)
    own, k_held, v_held = pl.pallas_call(
        functools.partial(suffix_kernel, c, heads),
        out_shape=[
            jax.ShapeDtypeStruct((rows + STATS, hd), bf),
            jax.ShapeDtypeStruct((keys, hd), bf),
            jax.ShapeDtypeStruct((keys, hd), bf),
        ],
        in_specs=[pl.BlockSpec(memory_space=pltpu.SMEM)] + whole(3) + [hbm, hbm],
        out_specs=whole(3),
        scratch_shapes=[pltpu.SemaphoreType.DMA((2,))],
        cost_estimate=pl.CostEstimate(
            flops=4 * rows * slots * hd,
            bytes_accessed=4 * forks * slots * hd,
            transcendentals=rows * slots,
        ),
        compiler_params=pltpu.CompilerParams(vmem_limit_bytes=6 * 2**20),
        name="suffix",
    )(
        lengths,
        q,
        sk.reshape(forks, slots, hd),
        sv.reshape(forks, slots, hd),
        k_own,
        v_own,
    )

    total = ring * rows
    f = jnp.float32

    def attend(kernel, n_in, key_count, packed, limit):
        state = [((total, TILE), f), ((total, 128), f)]
        outs = [((ring, rows + STATS, hd), bf)] if packed else state
        scratch = [((total, TILE), bf)] + [((total, key_count // 2), f)] * 2
        if packed:
            scratch += [state[1], state[0]]
        return pl.pallas_call(
            functools.partial(kernel, c),
            out_shape=[jax.ShapeDtypeStruct(*o) for o in outs],
            in_specs=whole(n_in),
            out_specs=whole(len(outs)),
            scratch_shapes=[VMEM(*x) for x in scratch],
            compiler_params=pltpu.CompilerParams(vmem_limit_bytes=limit * 2**20),
            cost_estimate=pl.CostEstimate(
                flops=4 * total * key_count * hd,
                bytes_accessed=4 * key_count * hd,
                transcendentals=total * key_count,
            ),
        )

    o1, m1 = attend(near_kernel, 5, 2 * keys, False, 20)(
        every, k_held, k_pair, v_held, v_pair
    )
    o1, m1, k_far, v_far = lax.optimization_barrier((o1, m1, k_far, v_far))
    k_far_pair = lax.ppermute(k_far, "core", swap)
    v_far_pair = lax.ppermute(v_far, "core", swap)
    o2, m2 = attend(next_kernel, 5, keys, False, 14)(every, k_far, v_far, o1, m1)
    (states,) = attend(far_kernel, 5, keys, True, 16)(
        every, k_far_pair, v_far_pair, o2, m2
    )

    got = lax.all_to_all(states, "z", 0, 0, tiled=True)
    att = pl.pallas_call(
        combine_kernel,
        out_shape=jax.ShapeDtypeStruct((chips, rows, hd), bf),
        in_specs=whole(2),
        out_specs=pl.BlockSpec(memory_space=VMEM),
        compiler_params=pltpu.CompilerParams(vmem_limit_bytes=4 * 2**20),
        name="combine",
    )(got, own)

    att = lax.all_to_all(att, CHIPS, 0, 0, tiled=True)
    other = lax.ppermute(att, "core", swap)
    core = lax.axis_index("core").astype(jnp.int32).reshape(1)
    mine = chips * 2 * forks // n_tp
    product = pl.pallas_call(
        functools.partial(project_kernel, heads, steps),
        out_shape=jax.ShapeDtypeStruct((n_tp, steps, mine, cols), bf),
        in_specs=[pl.BlockSpec(memory_space=pltpu.SMEM)] + whole(3),
        out_specs=pl.BlockSpec(memory_space=VMEM),
        scratch_shapes=[VMEM((chips * 2 * rows, hd), jnp.float32)],
        compiler_params=pltpu.CompilerParams(vmem_limit_bytes=10 * 2**20),
        name="project",
    )(core, att, other, w)
    parts = lax.all_to_all(product, TP, 0, 0, tiled=True)
    out = pl.pallas_call(
        sum_kernel,
        out_shape=jax.ShapeDtypeStruct((steps, mine, cols), bf),
        in_specs=whole(1),
        out_specs=pl.BlockSpec(memory_space=VMEM),
        compiler_params=pltpu.CompilerParams(vmem_limit_bytes=2 * 2**20),
        name="total",
    )(parts)
    return jnp.swapaxes(out, 0, 1)


def solution(mesh):
    fine = Mesh(
        mesh.devices.reshape(2, mesh.shape["ctx"] // 4, 2, 2, mesh.shape["tp"] // 2),
        CTX + TP,
    )
    return jax.shard_map(
        body,
        mesh=fine,
        in_specs=(
            P(CTX, None, TP, None),
            P(CTX, TP, None),
            P(CTX, TP, None),
            P(CTX, None, TP, None),
            P(CTX, None, TP, None),
            P(CTX),
            P(TP, CTX),
        ),
        out_specs=P(TP, None, CTX),
        check_vma=False,
    )
```

```python
import functools

import jax
import jax.numpy as jnp
from jax import lax
from jax.experimental import pallas as pl
from jax.experimental.pallas import tpu as pltpu
from jax._src.pallas.mosaic import core as pltpu_core
from jax.sharding import Mesh
from jax.sharding import PartitionSpec as P


CTX = ("xh", "z", "core")
CHIPS = ("xh", "z")
TP = ("xl", "y")
STATS = 8
NEG = -1e30
TILE = 256
UNROLL = 4
LOG2E = 1.4426950408889634
VMEM = pltpu.VMEM


def dot(a, b, ca, cb):
    return lax.dot_general(
        a, b, (((ca,), (cb,)), ((), ())), preferred_element_type=jnp.float32
    )


def shift_of(scores_max):
    hi = scores_max.astype(jnp.bfloat16)
    lo = (scores_max - hi.astype(jnp.float32)).astype(jnp.bfloat16)
    return hi, lo, hi.astype(jnp.float32) + lo.astype(jnp.float32)


def stat_rows(hi, lo, totals):
    rows = hi.shape[0]
    t_hi = totals.astype(jnp.bfloat16)
    t_lo = (totals - t_hi.astype(jnp.float32)).astype(jnp.bfloat16)
    lane = lax.broadcasted_iota(jnp.int32, (rows, 128), 1)
    f = jnp.float32
    table = jnp.where(
        lane == 0,
        hi.astype(f),
        jnp.where(
            lane == 1,
            lo.astype(f),
            jnp.where(lane == 2, t_hi.astype(f), jnp.where(lane == 3, t_lo.astype(f), 0.0)),
        ),
    ).astype(jnp.bfloat16)
    if rows < 128:
        table = jnp.concatenate([table, jnp.zeros((128 - rows, 128), jnp.bfloat16)], axis=0)
    pick = (
        lax.broadcasted_iota(jnp.int32, (STATS, 128), 0)
        == lax.broadcasted_iota(jnp.int32, (STATS, 128), 1)
    ).astype(jnp.bfloat16)
    return dot(pick, table, 1, 1).astype(jnp.bfloat16)


def accumulator(mxu, rows):
    return pltpu_core.AccMemorySpace(mxu)((rows, TILE), jnp.float32)


def scaled_queries(c, q_ref, q2):
    n, rows, hd = q_ref.shape
    f, bf = jnp.float32, jnp.bfloat16
    scaled = q_ref[...].reshape(n * rows, hd).astype(f) * c
    high = scaled.astype(bf)
    q2[:, :hd] = high
    q2[:, hd:] = (scaled - high.astype(f)).astype(bf)


def score_pass(q2, ks, scores, m_ref):
    keys = ks[0].shape[0]
    total = q2.shape[0]

    def body(*accs):
        @pl.loop(0, keys // TILE // UNROLL)
        def _(outer):
            for w in range(UNROLL):
                at = pl.ds(pl.multiple_of((outer * UNROLL + w) * TILE, TILE), TILE)
                for x in range(2):
                    k = ks[x][at, :]
                    pltpu.matmul_push_rhs(
                        jnp.concatenate([k, k], axis=1), w % 2, x, transpose=True
                    )
                for r in range(total // TILE):
                    rs = slice(r * TILE, (r + 1) * TILE)
                    for x in range(2):
                        pltpu.matmul_acc_lhs(
                            accs[2 * (r % 2) + x],
                            q2[rs, :],
                            load_staged_rhs=w % 2 if r == 0 else None,
                        )
                    tops = []
                    for x in range(2):
                        s = pltpu.matmul_pop(accs[2 * (r % 2) + x])
                        scores[x][rs, at] = s
                        tops.append(jnp.maximum(s[:, :128], s[:, 128:]))
                    m_ref[rs, :] = jnp.maximum(jnp.maximum(tops[0], tops[1]), m_ref[rs, :])

    pl.run_scoped(body, *[accumulator(i % 2, TILE) for i in range(4)])
    shift = shift_of(jnp.max(m_ref[...], axis=1, keepdims=True))[2]
    m_ref[...] = jnp.broadcast_to(shift, m_ref.shape)


def mix_pass(vs, scores, m_ref, o_ref):
    keys, hd = vs[0].shape
    total = m_ref.shape[0]
    parts = total // TILE
    bf = jnp.bfloat16
    ones = jnp.ones((TILE, TILE - hd), bf)

    def body(*accs):
        @pl.loop(0, keys // TILE // UNROLL)
        def _(outer):
            for w in range(UNROLL):
                at = pl.ds(pl.multiple_of((outer * UNROLL + w) * TILE, TILE), TILE)
                for x in range(2):
                    pltpu.matmul_push_rhs(
                        jnp.concatenate([vs[x][at, :], ones], axis=1), w % 2, x
                    )
                for u in range(parts):
                    rs = slice(u * TILE, (u + 1) * TILE)
                    m = m_ref[rs, :]
                    m = jnp.concatenate([m, m], axis=1)
                    for x in range(2):
                        p = jnp.exp2(scores[x][rs, at] - m).astype(bf)
                        pltpu.matmul_acc_lhs(
                            accs[x * parts + u], p, load_staged_rhs=w % 2 if u == 0 else None
                        )

        for u in range(parts):
            rs = slice(u * TILE, (u + 1) * TILE)
            o_ref[rs, :] = pltpu.matmul_pop(accs[u]) + pltpu.matmul_pop(accs[parts + u])

    pl.run_scoped(body, *[accumulator(i // parts, TILE) for i in range(2 * parts)])


def near_kernel(c, q_ref, ko_ref, kp_ref, vo_ref, vp_ref, o_ref, m_ref, q2, s_o, s_p):
    scaled_queries(c, q_ref, q2)
    m_ref[...] = jnp.full(m_ref.shape, -jnp.inf, jnp.float32)
    score_pass(q2, (ko_ref, kp_ref), (s_o, s_p), m_ref)
    mix_pass((vo_ref, vp_ref), (s_o, s_p), m_ref, o_ref)


def halves(ref):
    half = ref.shape[0] // 2
    return ref.at[:half], ref.at[half:]


def next_kernel(c, q_ref, k_ref, v_ref, o1_ref, m1_ref, o_ref, m_ref, q2, s_o, s_p):
    scaled_queries(c, q_ref, q2)
    m_ref[...] = m1_ref[...]
    score_pass(q2, halves(k_ref), (s_o, s_p), m_ref)
    mix_pass(halves(v_ref), (s_o, s_p), m_ref, o_ref)
    a = jnp.exp2(m1_ref[...] - m_ref[...])
    o_ref[...] = o_ref[...] + jnp.concatenate([a, a], axis=1) * o1_ref[...]


def far_kernel(
    c, q_ref, k_ref, v_ref, o1_ref, m1_ref, out_ref, q2, s_o, s_p, m_ref, o_ref
):
    n, rows, hd = q_ref.shape
    f, bf = jnp.float32, jnp.bfloat16
    scaled_queries(c, q_ref, q2)
    m_ref[...] = m1_ref[...]
    score_pass(q2, halves(k_ref), (s_o, s_p), m_ref)
    mix_pass(halves(v_ref), (s_o, s_p), m_ref, o_ref)

    lane = lax.broadcasted_iota(jnp.int32, (rows, 128), 1)
    table = jnp.zeros((rows, 128), f)
    for i in range(n):
        rs = slice(i * rows, (i + 1) * rows)
        m = m_ref[rs, :]
        a = jnp.exp2(m1_ref[rs, :] - m)
        out_ref[i, :rows, :] = (o_ref[rs, :hd] + a * o1_ref[rs, :hd]).astype(bf)
        t = o_ref[rs, hd:] + a * o1_ref[rs, hd:]
        hi, t_hi = m.astype(bf).astype(f), t.astype(bf).astype(f)
        for l, v in enumerate((hi, m - hi, t_hi, t - t_hi)):
            table = jnp.where(lane == STATS * i + l, v, table)
    turned = jnp.transpose(jnp.concatenate([table, jnp.zeros((128 - rows, 128), f)], axis=0))
    for i in range(n):
        out_ref[i, rows:, :] = turned[STATS * i : STATS * (i + 1)].astype(bf)


def hold_kernel(k_ref, v_ref, k_out, v_out, sems):
    get_k = pltpu.make_async_copy(k_ref, k_out, sems.at[0])
    get_v = pltpu.make_async_copy(v_ref, v_out, sems.at[1])
    get_k.start()
    get_v.start()
    get_k.wait()
    get_v.wait()


def suffix_kernel(c, heads, len_ref, q_ref, k_ref, v_ref, out_ref):
    forks, slots, _ = k_ref.shape
    rows = q_ref.shape[0] // forks
    his, los, tots = [], [], []
    for f in range(forks):
        q = q_ref[f * rows : (f + 1) * rows, :]
        s = dot(q, k_ref[f], 1, 1) * c
        step = lax.broadcasted_iota(jnp.int32, (rows, slots), 0) // heads
        slot = lax.broadcasted_iota(jnp.int32, (rows, slots), 1)
        s = jnp.where(slot < len_ref[f] + step + 1, s, NEG)
        hi, lo, shift = shift_of(jnp.max(s, axis=1, keepdims=True))
        p = jnp.exp2(s - shift)
        out_ref[f * rows : (f + 1) * rows, :] = dot(
            p.astype(jnp.bfloat16), v_ref[f], 1, 0
        ).astype(jnp.bfloat16)
        his.append(hi)
        los.append(lo)
        tots.append(jnp.sum(p, axis=1, keepdims=True))
    cat = functools.partial(jnp.concatenate, axis=0)
    out_ref[forks * rows :, :] = stat_rows(cat(his), cat(los), cat(tots))


def combine_kernel(got_ref, own_ref, out_ref):
    n = got_ref.shape[0]
    rows = own_ref.shape[0] - STATS
    f = jnp.float32
    m = got_ref[:, rows, :].astype(f) + got_ref[:, rows + 1, :].astype(f)
    t = got_ref[:, rows + 2, :].astype(f) + got_ref[:, rows + 3, :].astype(f)
    own = own_ref[rows:, :].astype(f)
    m_own = own[0:1] + own[1:2]
    t_own = own[2:3] + own[3:4]
    top = jnp.maximum(jnp.max(m, axis=0, keepdims=True), m_own)
    a = jnp.exp2(m - top)
    a_own = jnp.exp2(m_own - top)
    whole = jnp.sum(a * t, axis=0, keepdims=True) + a_own * t_own
    inv = 1.0 / whole
    table = jnp.concatenate(
        [a * inv, a_own * inv, jnp.zeros((128 - n - 1, 128), f)], axis=0
    )
    coef = jnp.transpose(table)
    acc = own_ref[:rows, :].astype(f) * coef[:rows, n : n + 1]
    for i in range(n):
        acc = acc + got_ref[i, :rows, :].astype(f) * coef[:rows, i : i + 1]
    att = acc.astype(jnp.bfloat16)
    for i in range(out_ref.shape[0]):
        out_ref[i] = att


def project_kernel(heads, steps, core_ref, own_ref, other_ref, w_ref, out_ref, x_ref):
    n, rows, hd = own_ref.shape
    core = core_ref[0]
    x4 = x_ref.reshape(n, 2, rows, hd)
    x4[:, core] = own_ref[...].astype(jnp.float32)
    x4[:, 1 - core] = other_ref[...].astype(jnp.float32)
    forks = n * 2 * rows // heads // steps
    acc = jnp.zeros((steps * forks, w_ref.shape[1]), jnp.float32)
    for h in range(0, heads, 2):
        pair = [
            jnp.concatenate(
                [
                    x_ref[pl.ds(s * heads + h + j, forks, stride=steps * heads), :]
                    for s in range(steps)
                ],
                axis=0,
            ).astype(jnp.bfloat16)
            for j in range(2)
        ]
        lhs = jnp.concatenate(pair, axis=1)
        acc = acc + dot(lhs, w_ref[h * hd : (h + 2) * hd, :], 1, 0)
    tps = out_ref.shape[0]
    mine = forks // tps
    for s in range(steps):
        block = acc[s * forks : (s + 1) * forks].astype(jnp.bfloat16)
        out_ref[:, s] = block.reshape(tps, mine, -1)


def sum_kernel(parts_ref, out_ref):
    out_ref[...] = jnp.sum(parts_ref[...].astype(jnp.float32), axis=0).astype(jnp.bfloat16)


def whole(n):
    return [pl.BlockSpec(memory_space=VMEM)] * n


def body(q, pk, pv, sk, sv, lengths, w):
    forks, steps, heads, hd = q.shape
    rows = forks * steps * heads
    keys = pk.shape[0]
    slots = sk.shape[1]
    c = hd**-0.5 * LOG2E
    chips = lax.axis_size(CHIPS)
    n_tp = lax.axis_size(TP)
    cols = w.shape[1]
    bf = jnp.bfloat16
    swap = [(0, 1), (1, 0)]

    k_own, v_own = pk.reshape(keys, hd), pv.reshape(keys, hd)
    k_far = lax.ppermute(k_own, "xh", swap)
    v_far = lax.ppermute(v_own, "xh", swap)
    k_pair = lax.ppermute(k_own, "core", swap)
    v_pair = lax.ppermute(v_own, "core", swap)
    q = q.reshape(rows, hd)
    ring = lax.axis_size("z")
    every = lax.all_to_all(
        jnp.broadcast_to(q[None], (ring, rows, hd)), "z", 0, 0, tiled=True
    )
    k_held, v_held = pl.pallas_call(
        hold_kernel,
        out_shape=[jax.ShapeDtypeStruct((keys, hd), bf)] * 2,
        in_specs=[pl.BlockSpec(memory_space=pltpu.HBM)] * 2,
        out_specs=whole(2),
        scratch_shapes=[pltpu.SemaphoreType.DMA((2,))],
        cost_estimate=pl.CostEstimate(
            flops=0, bytes_accessed=8 * keys * hd, transcendentals=0
        ),
        compiler_params=pltpu.CompilerParams(vmem_limit_bytes=2 * 2**20),
        name="hold",
    )(k_own, v_own)

    total = ring * rows
    f = jnp.float32

    def attend(kernel, n_in, key_count, packed, limit):
        state = [((total, TILE), f), ((total, 128), f)]
        outs = [((ring, rows + STATS, hd), bf)] if packed else state
        scratch = [((total, TILE), bf)] + [((total, key_count // 2), f)] * 2
        if packed:
            scratch += [state[1], state[0]]
        return pl.pallas_call(
            functools.partial(kernel, c),
            out_shape=[jax.ShapeDtypeStruct(*o) for o in outs],
            in_specs=whole(n_in),
            out_specs=whole(len(outs)),
            scratch_shapes=[VMEM(*x) for x in scratch],
            compiler_params=pltpu.CompilerParams(vmem_limit_bytes=limit * 2**20),
            cost_estimate=pl.CostEstimate(
                flops=4 * total * key_count * hd,
                bytes_accessed=4 * key_count * hd,
                transcendentals=total * key_count,
            ),
        )

    o1, m1 = attend(near_kernel, 5, 2 * keys, False, 20)(
        every, k_held, k_pair, v_held, v_pair
    )
    o1, m1, q_late = lax.optimization_barrier((o1, m1, q))
    own = pl.pallas_call(
        functools.partial(suffix_kernel, c, heads),
        out_shape=jax.ShapeDtypeStruct((rows + STATS, hd), bf),
        in_specs=[pl.BlockSpec(memory_space=pltpu.SMEM)] + whole(3),
        out_specs=pl.BlockSpec(memory_space=VMEM),
        cost_estimate=pl.CostEstimate(
            flops=4 * rows * slots * hd,
            bytes_accessed=4 * forks * slots * hd,
            transcendentals=rows * slots,
        ),
        compiler_params=pltpu.CompilerParams(vmem_limit_bytes=4 * 2**20),
        name="suffix",
    )(lengths, q_late, sk.reshape(forks, slots, hd), sv.reshape(forks, slots, hd))
    own, o1, m1, k_far, v_far = lax.optimization_barrier((own, o1, m1, k_far, v_far))
    k_far_pair = lax.ppermute(k_far, "core", swap)
    v_far_pair = lax.ppermute(v_far, "core", swap)
    o2, m2 = attend(next_kernel, 5, keys, False, 14)(every, k_far, v_far, o1, m1)
    (states,) = attend(far_kernel, 5, keys, True, 16)(
        every, k_far_pair, v_far_pair, o2, m2
    )

    got = lax.all_to_all(states, "z", 0, 0, tiled=True)
    att = pl.pallas_call(
        combine_kernel,
        out_shape=jax.ShapeDtypeStruct((chips, rows, hd), bf),
        in_specs=whole(2),
        out_specs=pl.BlockSpec(memory_space=VMEM),
        compiler_params=pltpu.CompilerParams(vmem_limit_bytes=4 * 2**20),
        name="combine",
    )(got, own)

    att = lax.all_to_all(att, CHIPS, 0, 0, tiled=True)
    other = lax.ppermute(att, "core", swap)
    core = lax.axis_index("core").astype(jnp.int32).reshape(1)
    mine = chips * 2 * forks // n_tp
    product = pl.pallas_call(
        functools.partial(project_kernel, heads, steps),
        out_shape=jax.ShapeDtypeStruct((n_tp, steps, mine, cols), bf),
        in_specs=[pl.BlockSpec(memory_space=pltpu.SMEM)] + whole(3),
        out_specs=pl.BlockSpec(memory_space=VMEM),
        scratch_shapes=[VMEM((chips * 2 * rows, hd), jnp.float32)],
        compiler_params=pltpu.CompilerParams(vmem_limit_bytes=10 * 2**20),
        name="project",
    )(core, att, other, w)
    parts = lax.all_to_all(product, TP, 0, 0, tiled=True)
    out = pl.pallas_call(
        sum_kernel,
        out_shape=jax.ShapeDtypeStruct((steps, mine, cols), bf),
        in_specs=whole(1),
        out_specs=pl.BlockSpec(memory_space=VMEM),
        compiler_params=pltpu.CompilerParams(vmem_limit_bytes=2 * 2**20),
        name="total",
    )(parts)
    return jnp.swapaxes(out, 0, 1)


def solution(mesh):
    fine = Mesh(
        mesh.devices.reshape(2, mesh.shape["ctx"] // 4, 2, 2, mesh.shape["tp"] // 2),
        CTX + TP,
    )
    return jax.shard_map(
        body,
        mesh=fine,
        in_specs=(
            P(CTX, None, TP, None),
            P(CTX, TP, None),
            P(CTX, TP, None),
            P(CTX, None, TP, None),
            P(CTX, None, TP, None),
            P(CTX),
            P(TP, CTX),
        ),
        out_specs=P(TP, None, CTX),
        check_vma=False,
    )
```

```python
import functools

import jax
import jax.numpy as jnp
from jax import lax
from jax.experimental import pallas as pl
from jax.experimental.pallas import tpu as pltpu
from jax._src.pallas.mosaic import core as pltpu_core
from jax.sharding import Mesh
from jax.sharding import PartitionSpec as P


CTX = ("xh", "z", "core")
CHIPS = ("xh", "z")
TP = ("xl", "y")
STATS = 8
NEG = -1e30
TILE = 256
UNROLL = 4
LOG2E = 1.4426950408889634
VMEM = pltpu.VMEM


def dot(a, b, ca, cb):
    return lax.dot_general(
        a, b, (((ca,), (cb,)), ((), ())), preferred_element_type=jnp.float32
    )


def shift_of(scores_max):
    hi = scores_max.astype(jnp.bfloat16)
    lo = (scores_max - hi.astype(jnp.float32)).astype(jnp.bfloat16)
    return hi, lo, hi.astype(jnp.float32) + lo.astype(jnp.float32)


def stat_rows(hi, lo, totals):
    rows = hi.shape[0]
    t_hi = totals.astype(jnp.bfloat16)
    t_lo = (totals - t_hi.astype(jnp.float32)).astype(jnp.bfloat16)
    lane = lax.broadcasted_iota(jnp.int32, (rows, 128), 1)
    f = jnp.float32
    table = jnp.where(
        lane == 0,
        hi.astype(f),
        jnp.where(
            lane == 1,
            lo.astype(f),
            jnp.where(lane == 2, t_hi.astype(f), jnp.where(lane == 3, t_lo.astype(f), 0.0)),
        ),
    ).astype(jnp.bfloat16)
    if rows < 128:
        table = jnp.concatenate([table, jnp.zeros((128 - rows, 128), jnp.bfloat16)], axis=0)
    pick = (
        lax.broadcasted_iota(jnp.int32, (STATS, 128), 0)
        == lax.broadcasted_iota(jnp.int32, (STATS, 128), 1)
    ).astype(jnp.bfloat16)
    return dot(pick, table, 1, 1).astype(jnp.bfloat16)


def accumulator(mxu, rows):
    return pltpu_core.AccMemorySpace(mxu)((rows, TILE), jnp.float32)


def scaled_queries(c, q_ref, q2):
    n, rows, hd = q_ref.shape
    f, bf = jnp.float32, jnp.bfloat16
    scaled = q_ref[...].reshape(n * rows, hd).astype(f) * c
    high = scaled.astype(bf)
    q2[:, :hd] = high
    q2[:, hd:] = (scaled - high.astype(f)).astype(bf)


def score_pass(q2, ks, scores, m_ref):
    keys = ks[0].shape[0]
    total = q2.shape[0]

    def body(*accs):
        @pl.loop(0, keys // TILE // UNROLL)
        def _(outer):
            for w in range(UNROLL):
                at = pl.ds(pl.multiple_of((outer * UNROLL + w) * TILE, TILE), TILE)
                for x in range(2):
                    k = ks[x][at, :]
                    pltpu.matmul_push_rhs(
                        jnp.concatenate([k, k], axis=1), w % 2, x, transpose=True
                    )
                for r in range(total // TILE):
                    rs = slice(r * TILE, (r + 1) * TILE)
                    for x in range(2):
                        pltpu.matmul_acc_lhs(
                            accs[2 * (r % 2) + x],
                            q2[rs, :],
                            load_staged_rhs=w % 2 if r == 0 else None,
                        )
                    tops = []
                    for x in range(2):
                        s = pltpu.matmul_pop(accs[2 * (r % 2) + x])
                        scores[x][rs, at] = s
                        tops.append(jnp.maximum(s[:, :128], s[:, 128:]))
                    m_ref[rs, :] = jnp.maximum(jnp.maximum(tops[0], tops[1]), m_ref[rs, :])

    pl.run_scoped(body, *[accumulator(i % 2, TILE) for i in range(4)])
    shift = shift_of(jnp.max(m_ref[...], axis=1, keepdims=True))[2]
    m_ref[...] = jnp.broadcast_to(shift, m_ref.shape)


def mix_pass(vs, scores, m_ref, o_ref):
    keys, hd = vs[0].shape
    total = m_ref.shape[0]
    parts = total // TILE
    bf = jnp.bfloat16
    ones = jnp.ones((TILE, TILE - hd), bf)

    def body(*accs):
        @pl.loop(0, keys // TILE // UNROLL)
        def _(outer):
            for w in range(UNROLL):
                at = pl.ds(pl.multiple_of((outer * UNROLL + w) * TILE, TILE), TILE)
                for x in range(2):
                    pltpu.matmul_push_rhs(
                        jnp.concatenate([vs[x][at, :], ones], axis=1), w % 2, x
                    )
                for u in range(parts):
                    rs = slice(u * TILE, (u + 1) * TILE)
                    m = m_ref[rs, :]
                    m = jnp.concatenate([m, m], axis=1)
                    for x in range(2):
                        p = jnp.exp2(scores[x][rs, at] - m).astype(bf)
                        pltpu.matmul_acc_lhs(
                            accs[x * parts + u], p, load_staged_rhs=w % 2 if u == 0 else None
                        )

        for u in range(parts):
            rs = slice(u * TILE, (u + 1) * TILE)
            o_ref[rs, :] = pltpu.matmul_pop(accs[u]) + pltpu.matmul_pop(accs[parts + u])

    pl.run_scoped(body, *[accumulator(i // parts, TILE) for i in range(2 * parts)])


def near_kernel(c, q_ref, ko_ref, kp_ref, vo_ref, vp_ref, o_ref, m_ref, q2, s_o, s_p):
    scaled_queries(c, q_ref, q2)
    m_ref[...] = jnp.full(m_ref.shape, -jnp.inf, jnp.float32)
    score_pass(q2, (ko_ref, kp_ref), (s_o, s_p), m_ref)
    mix_pass((vo_ref, vp_ref), (s_o, s_p), m_ref, o_ref)


def halves(ref):
    half = ref.shape[0] // 2
    return ref.at[:half], ref.at[half:]


def next_kernel(q2, k_ref, v_ref, o1_ref, m1_ref, o_ref, m_ref, s_o, s_p):
    m_ref[...] = m1_ref[...]
    score_pass(q2, halves(k_ref), (s_o, s_p), m_ref)
    mix_pass(halves(v_ref), (s_o, s_p), m_ref, o_ref)
    a = jnp.exp2(m1_ref[...] - m_ref[...])
    o_ref[...] = o_ref[...] + jnp.concatenate([a, a], axis=1) * o1_ref[...]


def far_kernel(
    q2, k_ref, v_ref, o1_ref, m1_ref, out_ref, s_o, s_p, m_ref, o_ref
):
    n, rows, hd = out_ref.shape[0], out_ref.shape[1] - STATS, v_ref.shape[1]
    f, bf = jnp.float32, jnp.bfloat16
    m_ref[...] = m1_ref[...]
    score_pass(q2, halves(k_ref), (s_o, s_p), m_ref)
    mix_pass(halves(v_ref), (s_o, s_p), m_ref, o_ref)

    lane = lax.broadcasted_iota(jnp.int32, (rows, 128), 1)
    table = jnp.zeros((rows, 128), f)
    for i in range(n):
        rs = slice(i * rows, (i + 1) * rows)
        m = m_ref[rs, :]
        a = jnp.exp2(m1_ref[rs, :] - m)
        out_ref[i, :rows, :] = (o_ref[rs, :hd] + a * o1_ref[rs, :hd]).astype(bf)
        t = o_ref[rs, hd:] + a * o1_ref[rs, hd:]
        hi, t_hi = m.astype(bf).astype(f), t.astype(bf).astype(f)
        for l, v in enumerate((hi, m - hi, t_hi, t - t_hi)):
            table = jnp.where(lane == STATS * i + l, v, table)
    turned = jnp.transpose(jnp.concatenate([table, jnp.zeros((128 - rows, 128), f)], axis=0))
    for i in range(n):
        out_ref[i, rows:, :] = turned[STATS * i : STATS * (i + 1)].astype(bf)


def hold_kernel(k_ref, v_ref, k_out, v_out, sems):
    get_k = pltpu.make_async_copy(k_ref, k_out, sems.at[0])
    get_v = pltpu.make_async_copy(v_ref, v_out, sems.at[1])
    get_k.start()
    get_v.start()
    get_k.wait()
    get_v.wait()


def suffix_kernel(c, heads, len_ref, q_ref, k_ref, v_ref, out_ref):
    forks, slots, _ = k_ref.shape
    rows = q_ref.shape[0] // forks
    his, los, tots = [], [], []
    for f in range(forks):
        q = q_ref[f * rows : (f + 1) * rows, :]
        s = dot(q, k_ref[f], 1, 1) * c
        step = lax.broadcasted_iota(jnp.int32, (rows, slots), 0) // heads
        slot = lax.broadcasted_iota(jnp.int32, (rows, slots), 1)
        s = jnp.where(slot < len_ref[f] + step + 1, s, NEG)
        hi, lo, shift = shift_of(jnp.max(s, axis=1, keepdims=True))
        p = jnp.exp2(s - shift)
        out_ref[f * rows : (f + 1) * rows, :] = dot(
            p.astype(jnp.bfloat16), v_ref[f], 1, 0
        ).astype(jnp.bfloat16)
        his.append(hi)
        los.append(lo)
        tots.append(jnp.sum(p, axis=1, keepdims=True))
    cat = functools.partial(jnp.concatenate, axis=0)
    out_ref[forks * rows :, :] = stat_rows(cat(his), cat(los), cat(tots))


def combine_kernel(got_ref, own_ref, out_ref):
    n = got_ref.shape[0]
    rows = own_ref.shape[0] - STATS
    f = jnp.float32
    m = got_ref[:, rows, :].astype(f) + got_ref[:, rows + 1, :].astype(f)
    t = got_ref[:, rows + 2, :].astype(f) + got_ref[:, rows + 3, :].astype(f)
    own = own_ref[rows:, :].astype(f)
    m_own = own[0:1] + own[1:2]
    t_own = own[2:3] + own[3:4]
    top = jnp.maximum(jnp.max(m, axis=0, keepdims=True), m_own)
    a = jnp.exp2(m - top)
    a_own = jnp.exp2(m_own - top)
    whole = jnp.sum(a * t, axis=0, keepdims=True) + a_own * t_own
    inv = 1.0 / whole
    table = jnp.concatenate(
        [a * inv, a_own * inv, jnp.zeros((128 - n - 1, 128), f)], axis=0
    )
    coef = jnp.transpose(table)
    acc = own_ref[:rows, :].astype(f) * coef[:rows, n : n + 1]
    for i in range(n):
        acc = acc + got_ref[i, :rows, :].astype(f) * coef[:rows, i : i + 1]
    att = acc.astype(jnp.bfloat16)
    for i in range(out_ref.shape[0]):
        out_ref[i] = att


def project_kernel(heads, steps, core_ref, own_ref, other_ref, w_ref, out_ref, x_ref):
    n, rows, hd = own_ref.shape
    core = core_ref[0]
    x4 = x_ref.reshape(n, 2, rows, hd)
    x4[:, core] = own_ref[...].astype(jnp.float32)
    x4[:, 1 - core] = other_ref[...].astype(jnp.float32)
    forks = n * 2 * rows // heads // steps
    acc = jnp.zeros((steps * forks, w_ref.shape[1]), jnp.float32)
    for h in range(0, heads, 2):
        pair = [
            jnp.concatenate(
                [
                    x_ref[pl.ds(s * heads + h + j, forks, stride=steps * heads), :]
                    for s in range(steps)
                ],
                axis=0,
            ).astype(jnp.bfloat16)
            for j in range(2)
        ]
        lhs = jnp.concatenate(pair, axis=1)
        acc = acc + dot(lhs, w_ref[h * hd : (h + 2) * hd, :], 1, 0)
    tps = out_ref.shape[0]
    mine = forks // tps
    for s in range(steps):
        block = acc[s * forks : (s + 1) * forks].astype(jnp.bfloat16)
        out_ref[:, s] = block.reshape(tps, mine, -1)


def sum_kernel(parts_ref, out_ref):
    out_ref[...] = jnp.sum(parts_ref[...].astype(jnp.float32), axis=0).astype(jnp.bfloat16)


def whole(n):
    return [pl.BlockSpec(memory_space=VMEM)] * n


def body(q, pk, pv, sk, sv, lengths, w):
    forks, steps, heads, hd = q.shape
    rows = forks * steps * heads
    keys = pk.shape[0]
    slots = sk.shape[1]
    c = hd**-0.5 * LOG2E
    chips = lax.axis_size(CHIPS)
    n_tp = lax.axis_size(TP)
    cols = w.shape[1]
    bf = jnp.bfloat16
    swap = [(0, 1), (1, 0)]

    k_own, v_own = pk.reshape(keys, hd), pv.reshape(keys, hd)
    k_far = lax.ppermute(k_own, "xh", swap)
    v_far = lax.ppermute(v_own, "xh", swap)
    k_pair = lax.ppermute(k_own, "core", swap)
    v_pair = lax.ppermute(v_own, "core", swap)
    q = q.reshape(rows, hd)
    ring = lax.axis_size("z")
    every = lax.all_to_all(
        jnp.broadcast_to(q[None], (ring, rows, hd)), "z", 0, 0, tiled=True
    )
    k_held, v_held = pl.pallas_call(
        hold_kernel,
        out_shape=[jax.ShapeDtypeStruct((keys, hd), bf)] * 2,
        in_specs=[pl.BlockSpec(memory_space=pltpu.HBM)] * 2,
        out_specs=whole(2),
        scratch_shapes=[pltpu.SemaphoreType.DMA((2,))],
        cost_estimate=pl.CostEstimate(
            flops=0, bytes_accessed=8 * keys * hd, transcendentals=0
        ),
        compiler_params=pltpu.CompilerParams(vmem_limit_bytes=2 * 2**20),
        name="hold",
    )(k_own, v_own)

    total = ring * rows
    f = jnp.float32

    def attend(kernel, n_in, key_count, kind, limit):
        state = [((total, TILE), f), ((total, 128), f)]
        scores = [((total, key_count // 2), f)] * 2
        outs, scratch = {
            "first": (state + [((total, TILE), bf)], scores),
            "next": (state, scores),
            "last": ([((ring, rows + STATS, hd), bf)], scores + state[::-1]),
        }[kind]
        return pl.pallas_call(
            kernel,
            out_shape=[jax.ShapeDtypeStruct(*o) for o in outs],
            in_specs=whole(n_in),
            out_specs=whole(len(outs)),
            scratch_shapes=[VMEM(*x) for x in scratch],
            compiler_params=pltpu.CompilerParams(vmem_limit_bytes=limit * 2**20),
            cost_estimate=pl.CostEstimate(
                flops=4 * total * key_count * hd,
                bytes_accessed=4 * key_count * hd,
                transcendentals=total * key_count,
            ),
        )

    o1, m1, q2 = attend(functools.partial(near_kernel, c), 5, 2 * keys, "first", 20)(
        every, k_held, k_pair, v_held, v_pair
    )
    o1, m1, q_late = lax.optimization_barrier((o1, m1, q))
    own = pl.pallas_call(
        functools.partial(suffix_kernel, c, heads),
        out_shape=jax.ShapeDtypeStruct((rows + STATS, hd), bf),
        in_specs=[pl.BlockSpec(memory_space=pltpu.SMEM)] + whole(3),
        out_specs=pl.BlockSpec(memory_space=VMEM),
        cost_estimate=pl.CostEstimate(
            flops=4 * rows * slots * hd,
            bytes_accessed=4 * forks * slots * hd,
            transcendentals=rows * slots,
        ),
        compiler_params=pltpu.CompilerParams(vmem_limit_bytes=4 * 2**20),
        name="suffix",
    )(lengths, q_late, sk.reshape(forks, slots, hd), sv.reshape(forks, slots, hd))
    own, o1, m1, k_far, v_far = lax.optimization_barrier((own, o1, m1, k_far, v_far))
    k_far_pair = lax.ppermute(k_far, "core", swap)
    v_far_pair = lax.ppermute(v_far, "core", swap)
    o2, m2 = attend(next_kernel, 5, keys, "next", 14)(q2, k_far, v_far, o1, m1)
    (states,) = attend(far_kernel, 5, keys, "last", 16)(
        q2, k_far_pair, v_far_pair, o2, m2
    )

    got = lax.all_to_all(states, "z", 0, 0, tiled=True)
    att = pl.pallas_call(
        combine_kernel,
        out_shape=jax.ShapeDtypeStruct((chips, rows, hd), bf),
        in_specs=whole(2),
        out_specs=pl.BlockSpec(memory_space=VMEM),
        compiler_params=pltpu.CompilerParams(vmem_limit_bytes=4 * 2**20),
        name="combine",
    )(got, own)

    att = lax.all_to_all(att, CHIPS, 0, 0, tiled=True)
    other = lax.ppermute(att, "core", swap)
    core = lax.axis_index("core").astype(jnp.int32).reshape(1)
    mine = chips * 2 * forks // n_tp
    product = pl.pallas_call(
        functools.partial(project_kernel, heads, steps),
        out_shape=jax.ShapeDtypeStruct((n_tp, steps, mine, cols), bf),
        in_specs=[pl.BlockSpec(memory_space=pltpu.SMEM)] + whole(3),
        out_specs=pl.BlockSpec(memory_space=VMEM),
        scratch_shapes=[VMEM((chips * 2 * rows, hd), jnp.float32)],
        compiler_params=pltpu.CompilerParams(vmem_limit_bytes=10 * 2**20),
        name="project",
    )(core, att, other, w)
    parts = lax.all_to_all(product, TP, 0, 0, tiled=True)
    out = pl.pallas_call(
        sum_kernel,
        out_shape=jax.ShapeDtypeStruct((steps, mine, cols), bf),
        in_specs=whole(1),
        out_specs=pl.BlockSpec(memory_space=VMEM),
        compiler_params=pltpu.CompilerParams(vmem_limit_bytes=2 * 2**20),
        name="total",
    )(parts)
    return jnp.swapaxes(out, 0, 1)


def solution(mesh):
    fine = Mesh(
        mesh.devices.reshape(2, mesh.shape["ctx"] // 4, 2, 2, mesh.shape["tp"] // 2),
        CTX + TP,
    )
    return jax.shard_map(
        body,
        mesh=fine,
        in_specs=(
            P(CTX, None, TP, None),
            P(CTX, TP, None),
            P(CTX, TP, None),
            P(CTX, None, TP, None),
            P(CTX, None, TP, None),
            P(CTX),
            P(TP, CTX),
        ),
        out_specs=P(TP, None, CTX),
        check_vma=False,
    )
```

```python
import functools

import jax
import jax.numpy as jnp
from jax import lax
from jax.experimental import pallas as pl
from jax.experimental.pallas import tpu as pltpu
from jax._src.pallas.mosaic import core as pltpu_core
from jax.sharding import Mesh
from jax.sharding import PartitionSpec as P


CTX = ("xh", "z", "core")
CHIPS = ("xh", "z")
TP = ("xl", "y")
STATS = 8
NEG = -1e30
TILE = 256
UNROLL = 4
LOG2E = 1.4426950408889634
VMEM = pltpu.VMEM


def dot(a, b, ca, cb):
    return lax.dot_general(
        a, b, (((ca,), (cb,)), ((), ())), preferred_element_type=jnp.float32
    )


def shift_of(scores_max):
    hi = scores_max.astype(jnp.bfloat16)
    lo = (scores_max - hi.astype(jnp.float32)).astype(jnp.bfloat16)
    return hi, lo, hi.astype(jnp.float32) + lo.astype(jnp.float32)


def stat_rows(hi, lo, totals):
    rows = hi.shape[0]
    t_hi = totals.astype(jnp.bfloat16)
    t_lo = (totals - t_hi.astype(jnp.float32)).astype(jnp.bfloat16)
    lane = lax.broadcasted_iota(jnp.int32, (rows, 128), 1)
    f = jnp.float32
    table = jnp.where(
        lane == 0,
        hi.astype(f),
        jnp.where(
            lane == 1,
            lo.astype(f),
            jnp.where(lane == 2, t_hi.astype(f), jnp.where(lane == 3, t_lo.astype(f), 0.0)),
        ),
    ).astype(jnp.bfloat16)
    if rows < 128:
        table = jnp.concatenate([table, jnp.zeros((128 - rows, 128), jnp.bfloat16)], axis=0)
    pick = (
        lax.broadcasted_iota(jnp.int32, (STATS, 128), 0)
        == lax.broadcasted_iota(jnp.int32, (STATS, 128), 1)
    ).astype(jnp.bfloat16)
    return dot(pick, table, 1, 1).astype(jnp.bfloat16)


def accumulator(mxu, rows):
    return pltpu_core.AccMemorySpace(mxu)((rows, TILE), jnp.float32)


def scaled_queries(c, q_ref, q2):
    n, rows, hd = q_ref.shape
    f, bf = jnp.float32, jnp.bfloat16
    scaled = q_ref[...].reshape(n * rows, hd).astype(f) * c
    high = scaled.astype(bf)
    q2[:, :hd] = high
    q2[:, hd:] = (scaled - high.astype(f)).astype(bf)


def score_pass(q2, ks, scores, m_ref):
    keys = ks[0].shape[0]
    total = q2.shape[0]

    def body(*accs):
        @pl.loop(0, keys // TILE // UNROLL)
        def _(outer):
            for w in range(UNROLL):
                at = pl.ds(pl.multiple_of((outer * UNROLL + w) * TILE, TILE), TILE)
                for x in range(2):
                    k = ks[x][at, :]
                    pltpu.matmul_push_rhs(
                        jnp.concatenate([k, k], axis=1), w % 2, x, transpose=True
                    )
                for r in range(total // TILE):
                    rs = slice(r * TILE, (r + 1) * TILE)
                    for x in range(2):
                        pltpu.matmul_acc_lhs(
                            accs[2 * (r % 2) + x],
                            q2[rs, :],
                            load_staged_rhs=w % 2 if r == 0 else None,
                        )
                    tops = []
                    for x in range(2):
                        s = pltpu.matmul_pop(accs[2 * (r % 2) + x])
                        scores[x][rs, at] = s
                        tops.append(jnp.maximum(s[:, :128], s[:, 128:]))
                    m_ref[rs, :] = jnp.maximum(jnp.maximum(tops[0], tops[1]), m_ref[rs, :])

    pl.run_scoped(body, *[accumulator(i % 2, TILE) for i in range(4)])
    shift = shift_of(jnp.max(m_ref[...], axis=1, keepdims=True))[2]
    m_ref[...] = jnp.broadcast_to(shift, m_ref.shape)


def mix_pass(vs, scores, m_ref, o_ref):
    keys, hd = vs[0].shape
    total = m_ref.shape[0]
    parts = total // TILE
    bf = jnp.bfloat16
    ones = jnp.ones((TILE, TILE - hd), bf)

    def body(*accs):
        @pl.loop(0, keys // TILE // UNROLL)
        def _(outer):
            for w in range(UNROLL):
                at = pl.ds(pl.multiple_of((outer * UNROLL + w) * TILE, TILE), TILE)
                for x in range(2):
                    pltpu.matmul_push_rhs(
                        jnp.concatenate([vs[x][at, :], ones], axis=1), w % 2, x
                    )
                for u in range(parts):
                    rs = slice(u * TILE, (u + 1) * TILE)
                    m = m_ref[rs, :]
                    m = jnp.concatenate([m, m], axis=1)
                    for x in range(2):
                        p = jnp.exp2(scores[x][rs, at] - m).astype(bf)
                        pltpu.matmul_acc_lhs(
                            accs[x * parts + u], p, load_staged_rhs=w % 2 if u == 0 else None
                        )

        for u in range(parts):
            rs = slice(u * TILE, (u + 1) * TILE)
            o_ref[rs, :] = pltpu.matmul_pop(accs[u]) + pltpu.matmul_pop(accs[parts + u])

    pl.run_scoped(body, *[accumulator(i // parts, TILE) for i in range(2 * parts)])


def near_kernel(c, q_ref, ko_ref, kp_ref, vo_ref, vp_ref, o_ref, m_ref, q2, s_o, s_p):
    scaled_queries(c, q_ref, q2)
    m_ref[...] = jnp.full(m_ref.shape, -jnp.inf, jnp.float32)
    score_pass(q2, (ko_ref, kp_ref), (s_o, s_p), m_ref)
    mix_pass((vo_ref, vp_ref), (s_o, s_p), m_ref, o_ref)


def halves(ref):
    half = ref.shape[0] // 2
    return ref.at[:half], ref.at[half:]


def next_kernel(q2, k_ref, v_ref, o1_ref, m1_ref, o_ref, m_ref, s_o, s_p):
    m_ref[...] = m1_ref[...]
    score_pass(q2, halves(k_ref), (s_o, s_p), m_ref)
    mix_pass(halves(v_ref), (s_o, s_p), m_ref, o_ref)
    a = jnp.exp2(m1_ref[...] - m_ref[...])
    o_ref[...] = o_ref[...] + jnp.concatenate([a, a], axis=1) * o1_ref[...]


def far_kernel(
    q2, k_ref, v_ref, o1_ref, m1_ref, out_ref, s_o, s_p, m_ref, o_ref
):
    n, rows, hd = out_ref.shape[0], out_ref.shape[1] - STATS, v_ref.shape[1]
    f, bf = jnp.float32, jnp.bfloat16
    m_ref[...] = m1_ref[...]
    score_pass(q2, halves(k_ref), (s_o, s_p), m_ref)
    mix_pass(halves(v_ref), (s_o, s_p), m_ref, o_ref)

    lane = lax.broadcasted_iota(jnp.int32, (rows, 128), 1)
    table = jnp.zeros((rows, 128), f)
    for i in range(n):
        rs = slice(i * rows, (i + 1) * rows)
        m = m_ref[rs, :]
        a = jnp.exp2(m1_ref[rs, :] - m)
        out_ref[i, :rows, :] = (o_ref[rs, :hd] + a * o1_ref[rs, :hd]).astype(bf)
        t = o_ref[rs, hd:] + a * o1_ref[rs, hd:]
        hi, t_hi = m.astype(bf).astype(f), t.astype(bf).astype(f)
        for l, v in enumerate((hi, m - hi, t_hi, t - t_hi)):
            table = jnp.where(lane == STATS * i + l, v, table)
    turned = jnp.transpose(jnp.concatenate([table, jnp.zeros((128 - rows, 128), f)], axis=0))
    for i in range(n):
        out_ref[i, rows:, :] = turned[STATS * i : STATS * (i + 1)].astype(bf)


def hold_kernel(k_ref, v_ref, k_out, v_out, sems):
    get_k = pltpu.make_async_copy(k_ref, k_out, sems.at[0])
    get_v = pltpu.make_async_copy(v_ref, v_out, sems.at[1])
    get_k.start()
    get_v.start()
    get_k.wait()
    get_v.wait()


def suffix_kernel(c, heads, len_ref, q_ref, k_ref, v_ref, out_ref):
    forks, slots, _ = k_ref.shape
    rows = q_ref.shape[0] // forks
    his, los, tots = [], [], []
    for f in range(forks):
        q = q_ref[f * rows : (f + 1) * rows, :]
        s = dot(q, k_ref[f], 1, 1) * c
        step = lax.broadcasted_iota(jnp.int32, (rows, slots), 0) // heads
        slot = lax.broadcasted_iota(jnp.int32, (rows, slots), 1)
        s = jnp.where(slot < len_ref[f] + step + 1, s, NEG)
        hi, lo, shift = shift_of(jnp.max(s, axis=1, keepdims=True))
        p = jnp.exp2(s - shift)
        out_ref[f * rows : (f + 1) * rows, :] = dot(
            p.astype(jnp.bfloat16), v_ref[f], 1, 0
        ).astype(jnp.bfloat16)
        his.append(hi)
        los.append(lo)
        tots.append(jnp.sum(p, axis=1, keepdims=True))
    cat = functools.partial(jnp.concatenate, axis=0)
    out_ref[forks * rows :, :] = stat_rows(cat(his), cat(los), cat(tots))


def combine_kernel(got_ref, own_ref, out_ref):
    n = got_ref.shape[0]
    rows = own_ref.shape[0] - STATS
    f = jnp.float32
    m = got_ref[:, rows, :].astype(f) + got_ref[:, rows + 1, :].astype(f)
    t = got_ref[:, rows + 2, :].astype(f) + got_ref[:, rows + 3, :].astype(f)
    own = own_ref[rows:, :].astype(f)
    m_own = own[0:1] + own[1:2]
    t_own = own[2:3] + own[3:4]
    top = jnp.maximum(jnp.max(m, axis=0, keepdims=True), m_own)
    a = jnp.exp2(m - top)
    a_own = jnp.exp2(m_own - top)
    whole = jnp.sum(a * t, axis=0, keepdims=True) + a_own * t_own
    inv = 1.0 / whole
    table = jnp.concatenate(
        [a * inv, a_own * inv, jnp.zeros((128 - n - 1, 128), f)], axis=0
    )
    coef = jnp.transpose(table)
    acc = own_ref[:rows, :].astype(f) * coef[:rows, n : n + 1]
    for i in range(n):
        acc = acc + got_ref[i, :rows, :].astype(f) * coef[:rows, i : i + 1]
    att = acc.astype(jnp.bfloat16)
    for i in range(out_ref.shape[0]):
        out_ref[i] = att


def project_kernel(heads, steps, core_ref, own_ref, other_ref, w_ref, out_ref, x_ref):
    n, rows, hd = own_ref.shape
    core = core_ref[0]
    x4 = x_ref.reshape(n, 2, rows, hd)
    x4[:, core] = own_ref[...].astype(jnp.float32)
    x4[:, 1 - core] = other_ref[...].astype(jnp.float32)
    forks = n * 2 * rows // heads // steps
    lhs = [
        jnp.concatenate(
            [
                x_ref[pl.ds(s * heads + h, forks, stride=steps * heads), :]
                for s in range(steps)
            ],
            axis=0,
        ).astype(jnp.bfloat16)
        for h in range(heads)
    ]
    acc = dot(jnp.concatenate(lhs, axis=1), w_ref[...], 1, 0)
    tps = out_ref.shape[0]
    mine = forks // tps
    for s in range(steps):
        block = acc[s * forks : (s + 1) * forks].astype(jnp.bfloat16)
        out_ref[:, s] = block.reshape(tps, mine, -1)


def sum_kernel(parts_ref, out_ref):
    out_ref[...] = jnp.sum(parts_ref[...].astype(jnp.float32), axis=0).astype(jnp.bfloat16)


def whole(n):
    return [pl.BlockSpec(memory_space=VMEM)] * n


def body(q, pk, pv, sk, sv, lengths, w):
    forks, steps, heads, hd = q.shape
    rows = forks * steps * heads
    keys = pk.shape[0]
    slots = sk.shape[1]
    c = hd**-0.5 * LOG2E
    chips = lax.axis_size(CHIPS)
    n_tp = lax.axis_size(TP)
    cols = w.shape[1]
    bf = jnp.bfloat16
    swap = [(0, 1), (1, 0)]

    k_own, v_own = pk.reshape(keys, hd), pv.reshape(keys, hd)
    k_far = lax.ppermute(k_own, "xh", swap)
    v_far = lax.ppermute(v_own, "xh", swap)
    k_pair = lax.ppermute(k_own, "core", swap)
    v_pair = lax.ppermute(v_own, "core", swap)
    q = q.reshape(rows, hd)
    ring = lax.axis_size("z")
    every = lax.all_to_all(
        jnp.broadcast_to(q[None], (ring, rows, hd)), "z", 0, 0, tiled=True
    )
    k_held, v_held = pl.pallas_call(
        hold_kernel,
        out_shape=[jax.ShapeDtypeStruct((keys, hd), bf)] * 2,
        in_specs=[pl.BlockSpec(memory_space=pltpu.HBM)] * 2,
        out_specs=whole(2),
        scratch_shapes=[pltpu.SemaphoreType.DMA((2,))],
        cost_estimate=pl.CostEstimate(
            flops=0, bytes_accessed=8 * keys * hd, transcendentals=0
        ),
        compiler_params=pltpu.CompilerParams(vmem_limit_bytes=2 * 2**20),
        name="hold",
    )(k_own, v_own)

    total = ring * rows
    f = jnp.float32

    def attend(kernel, n_in, key_count, kind, limit):
        state = [((total, TILE), f), ((total, 128), f)]
        scores = [((total, key_count // 2), f)] * 2
        outs, scratch = {
            "first": (state + [((total, TILE), bf)], scores),
            "next": (state, scores),
            "last": ([((ring, rows + STATS, hd), bf)], scores + state[::-1]),
        }[kind]
        return pl.pallas_call(
            kernel,
            out_shape=[jax.ShapeDtypeStruct(*o) for o in outs],
            in_specs=whole(n_in),
            out_specs=whole(len(outs)),
            scratch_shapes=[VMEM(*x) for x in scratch],
            compiler_params=pltpu.CompilerParams(vmem_limit_bytes=limit * 2**20),
            cost_estimate=pl.CostEstimate(
                flops=4 * total * key_count * hd,
                bytes_accessed=4 * key_count * hd,
                transcendentals=total * key_count,
            ),
        )

    o1, m1, q2 = attend(functools.partial(near_kernel, c), 5, 2 * keys, "first", 20)(
        every, k_held, k_pair, v_held, v_pair
    )
    o1, m1, q_late = lax.optimization_barrier((o1, m1, q))
    own = pl.pallas_call(
        functools.partial(suffix_kernel, c, heads),
        out_shape=jax.ShapeDtypeStruct((rows + STATS, hd), bf),
        in_specs=[pl.BlockSpec(memory_space=pltpu.SMEM)] + whole(3),
        out_specs=pl.BlockSpec(memory_space=VMEM),
        cost_estimate=pl.CostEstimate(
            flops=4 * rows * slots * hd,
            bytes_accessed=4 * forks * slots * hd,
            transcendentals=rows * slots,
        ),
        compiler_params=pltpu.CompilerParams(vmem_limit_bytes=4 * 2**20),
        name="suffix",
    )(lengths, q_late, sk.reshape(forks, slots, hd), sv.reshape(forks, slots, hd))
    own, o1, m1, k_far, v_far = lax.optimization_barrier((own, o1, m1, k_far, v_far))
    k_far_pair = lax.ppermute(k_far, "core", swap)
    v_far_pair = lax.ppermute(v_far, "core", swap)
    o2, m2 = attend(next_kernel, 5, keys, "next", 14)(q2, k_far, v_far, o1, m1)
    (states,) = attend(far_kernel, 5, keys, "last", 16)(
        q2, k_far_pair, v_far_pair, o2, m2
    )

    got = lax.all_to_all(states, "z", 0, 0, tiled=True)
    att = pl.pallas_call(
        combine_kernel,
        out_shape=jax.ShapeDtypeStruct((chips, rows, hd), bf),
        in_specs=whole(2),
        out_specs=pl.BlockSpec(memory_space=VMEM),
        compiler_params=pltpu.CompilerParams(vmem_limit_bytes=4 * 2**20),
        name="combine",
    )(got, own)

    att = lax.all_to_all(att, CHIPS, 0, 0, tiled=True)
    other = lax.ppermute(att, "core", swap)
    core = lax.axis_index("core").astype(jnp.int32).reshape(1)
    mine = chips * 2 * forks // n_tp
    product = pl.pallas_call(
        functools.partial(project_kernel, heads, steps),
        out_shape=jax.ShapeDtypeStruct((n_tp, steps, mine, cols), bf),
        in_specs=[pl.BlockSpec(memory_space=pltpu.SMEM)] + whole(3),
        out_specs=pl.BlockSpec(memory_space=VMEM),
        scratch_shapes=[VMEM((chips * 2 * rows, hd), jnp.float32)],
        compiler_params=pltpu.CompilerParams(vmem_limit_bytes=10 * 2**20),
        name="project",
    )(core, att, other, w)
    parts = lax.all_to_all(product, TP, 0, 0, tiled=True)
    out = pl.pallas_call(
        sum_kernel,
        out_shape=jax.ShapeDtypeStruct((steps, mine, cols), bf),
        in_specs=whole(1),
        out_specs=pl.BlockSpec(memory_space=VMEM),
        compiler_params=pltpu.CompilerParams(vmem_limit_bytes=2 * 2**20),
        name="total",
    )(parts)
    return jnp.swapaxes(out, 0, 1)


def solution(mesh):
    fine = Mesh(
        mesh.devices.reshape(2, mesh.shape["ctx"] // 4, 2, 2, mesh.shape["tp"] // 2),
        CTX + TP,
    )
    return jax.shard_map(
        body,
        mesh=fine,
        in_specs=(
            P(CTX, None, TP, None),
            P(CTX, TP, None),
            P(CTX, TP, None),
            P(CTX, None, TP, None),
            P(CTX, None, TP, None),
            P(CTX),
            P(TP, CTX),
        ),
        out_specs=P(TP, None, CTX),
        check_vma=False,
    )
```
